32 devices in a mesh: grp: 2 (over y), row: 4 (over z), col: 4 (over x, core).
Axes of the slice: x: 2, y: 2, z: 4, core: 2. Of those that a mesh axis runs over, the one named last changes fastest.
Arguments:
- factor: float32 [4, 1024, 1024], P('grp', ('row', 'col')), may hold values from -0.1875 to 0.1875
- pivots: float32 [4, 1024], P('grp', ('row', 'col')), may hold values from 0.5 to 2
- constraints: float32 [4, 1024, 4096], P('grp', None, ('col', 'row')), may hold values from -0.09375 to 0.09375
Outputs:
- q_panels: float32 [4, 1024, 4096], P('row', 'grp', 'col')
The draws below stay inside these ranges and needn't reach their ends.
All inputs are finite; a program needn't handle non-finite values.
Results may differ from the reference program's by a relative error of at most 0.0011.
Values may be sent and summed in bfloat16 or wider, within the bound.
A program may use at most 64 MiB of HBM per device.

```python
import math
import jax
import jax.numpy as jnp
from jax import lax

M = 1024
N = 4096
NBLK = 4
STRIP = 256
N_ROW = 4
N_COL = 4


def steps_of(own_key, extent, shards, low, top_value):
    factor_of = 1.0
    for axis_at, blocks in shards:
        draws = jax.random.uniform(jax.random.fold_in(jax.random.fold_in(own_key, 6), axis_at), (blocks,), jnp.float32, low / len(shards), top_value / len(shards))
        factor_of = factor_of * jnp.repeat(jnp.exp(draws), extent[axis_at] // blocks).reshape((-1,) + (1,) * (len(extent) - 1 - axis_at))
    return factor_of


def gaussian(own_key, shape, scale, reach, pieces=(), held_as=jnp.bfloat16):
    drawn = scale * jax.random.normal(own_key, shape, jnp.float32)
    if pieces:
        drawn = drawn * steps_of(own_key, shape, pieces, -0.22, 0.18)
    return jnp.clip(drawn, -reach, reach).astype(held_as)


def setup_inputs(seed: int = 0) -> dict:
    keys = jax.random.split(jax.random.key(seed), 4)
    return {
        "factor": gaussian(keys[0], (NBLK, M, M), (1.0 / M ** 0.5), 0.1875, ((0, 2), (1, 16)), jnp.float32),
        "pivots": jnp.clip(jnp.exp(math.log(2.0) - 1.3862944 * jax.random.uniform(keys[1], (NBLK, M), jnp.float32) ** steps_of(keys[1], (NBLK, M), ((0, 2), (1, 16)), -0.2, 0.2)), 0.5, 2.0),
        "constraints": gaussian(keys[2], (NBLK, M, N), (1.0 / (M * NBLK) ** 0.5), 0.09375, ((0, 2), (2, 16)), jnp.float32),
    }


def reference(factor, pivots, constraints):
    positions = jnp.arange(M, dtype=jnp.int32)
    strict_lower = positions[None, :] < positions[:, None]

    def one_block(running, block_items):
        factor_rows, pivot_rows, right_side = block_items
        triangle = jnp.where(strict_lower, factor_rows, jnp.zeros_like(factor_rows)) + jnp.diag(pivot_rows)
        projected = jnp.dot(triangle, right_side, precision=lax.Precision.HIGHEST, preferred_element_type=jnp.float32).astype(jnp.bfloat16)
        product = lax.dot_general(projected, projected, (((0,), (0,)), ((), ())), preferred_element_type=jnp.float32)
        return running + product, None

    running, leftover = lax.scan(one_block, jnp.zeros((N, N), jnp.float32), (factor, pivots, constraints))
    regrouped = running.reshape(N_COL, N_ROW, STRIP, N).transpose(1, 0, 2, 3)
    return regrouped.reshape(N_ROW, N // N_ROW, N)
```

```python
import functools
import jax
import jax.numpy as jnp
from jax import lax
from jax.experimental import pallas as pl
from jax.experimental.pallas import tpu as pltpu
from jax.sharding import PartitionSpec as P

MESH = pl.DeviceIdType.MESH
f32 = jnp.float32
bf16 = jnp.bfloat16
W = 256


H = W // 2
GAIN = 8192.0


def encode(t):
    a = t * GAIN
    return (a * jnp.abs(a) * (a * a)).astype(bf16)


def decode(w):
    a = w.astype(f32)
    root = jnp.sqrt(jnp.sqrt(jnp.abs(a))) * (1.0 / GAIN)
    return jnp.where(a < 0, -root, root)


def order(zz, j):
    if j == 0:
        return zz
    if j == 1:
        return zz - 1 + 2 * ((3 - zz) // 3)
    if j == 2:
        return zz + 1 + (3 - zz) // 3 - 3 * (zz // 3)
    return 3 - 3 * (zz // 2)


def paired(nb, fac, piv, c_hbm, out, tbuf, cbuf, chi, clo, acc, colbuf, rowt, rowe, obuf, sbuf, rbuf,
           dsb, drb, yrb, csem, tss, trs, pis, pir, pfs, pfr, pxs, pxr, res, rer, rcs, rcr, rss, rsr,
           dms, dmr, yfs, yfr, osem):
    g, z, c = lax.axis_index("grp"), lax.axis_index("row"), lax.axis_index("col")
    sib = c + 1 - 2 * (c % 2)
    xn = (c + 2) % 4
    xs = (sib + 2) % 4
    xp = c // 2
    d_up, d_dn = (g, z + 1, c), (g, z - 1, c)
    d_xn, d_sib = (g, z, xn), (g, z, sib)
    d_y = (1 - g, z, c)
    e = 3 * (z // 2)
    f = 3 - e
    o = 3 - z
    d_in = (g, z + 1 - 2 * (z // 2), c)
    d_end = (g, e, c)
    is_mid = (z == 1) | (z == 2)
    is_end = (z == 0) | (z == 3)
    piece = fac.shape[1]

    cload = pltpu.make_async_copy(c_hbm, cbuf, csem)
    cload.start()

    bar = pltpu.get_barrier_semaphore()

    def hello(dev):
        pl.semaphore_signal(bar, inc=1, device_id=dev, device_id_type=MESH)

    hello(d_xn)
    hello(d_sib)
    hello(d_y)

    @pl.when(z < 3)
    def _():
        hello(d_up)

    @pl.when(z > 0)
    def _():
        hello(d_dn)

    for kc in range(4):
        @pl.when(kc <= z)
        def _():
            start = W * z + piece * c
            rows = start + lax.broadcasted_iota(jnp.int32, (piece, W), 0)
            cols = W * kc + lax.broadcasted_iota(jnp.int32, (piece, W), 1)
            for b in range(nb):
                diag = jnp.where(cols == rows, jnp.broadcast_to(piv[b:b + 1, :], (piece, W)), 0.0)
                tbuf[kc, b, pl.ds(pl.multiple_of(start, piece), piece), :] = jnp.where(
                    cols < rows, fac[b, :, W * kc:W * (kc + 1)], diag)

    pl.semaphore_wait(bar, 3 + (z + 3) // 4 + 1 - z // 3)

    def remote(src, dst, ss, rs, dev):
        return pltpu.make_async_remote_copy(
            src_ref=src, dst_ref=dst, send_sem=ss, recv_sem=rs, device_id=dev, device_id_type=MESH)

    def tcopy(route, arrive, r, kc, col, dev):
        ref = tbuf.at[kc, :, pl.ds(pl.multiple_of(W * r + piece * col, piece), piece), :]
        return remote(ref, ref, tss.at[route, r, kc], trs.at[arrive, r, kc], dev)

    def t_up(r, kc):
        return tcopy(0, 0, r, kc, c, d_up)

    def t_dn(r, kc):
        return tcopy(1, 0, r, kc, c, d_dn)

    def t_xn(r, kc):
        return tcopy(2, 1, r, kc, c, d_xn)

    def t_sib(r, kc):
        return tcopy(3, 2, r, kc, c, d_sib)

    def t_fwd(r, kc):
        return tcopy(4, 3, r, kc, xn, d_sib)

    def t_first(j):
        r = order(z, j)

        @pl.loop(0, r + 1)
        def _(kc):
            if j > 0:
                t_up(r, kc).wait_recv()

            @pl.when((r <= z) & (z < 3))
            def _():
                t_up(r, kc).start()

            @pl.when((r >= z) & (z > 0))
            def _():
                t_dn(r, kc).start()

            t_xn(r, kc).start()
            t_sib(r, kc).start()

    def t_second(j):
        r = order(z, j)

        @pl.loop(0, r + 1)
        def _(kc):
            t_xn(r, kc).wait_recv()
            t_fwd(r, kc).start()

    def pin(s, r):
        return remote(colbuf.at[s, r], colbuf.at[s, r], pis.at[r], pir.at[s, r], d_in)

    def pfwd(s, r, h):
        ref = colbuf.at[s, r, :, H * h:H * (h + 1)]
        return remote(ref, ref, pfs.at[r, h], pfr.at[r, h], d_in)

    def px(route, col, r):
        ref = rowt.at[col, r]
        return remote(ref, ref, pxs.at[route, r], pxr.at[route, r], d_xn if route == 0 else d_sib)

    def rup(r):
        return remote(rowt.at[xn, r], rowe.at[xn, r], res.at[r], rer.at[r], d_in)

    def rshare(route, col, r):
        ref = rowe.at[col, r]
        return remote(ref, ref, rcs.at[route, r], rcr.at[route, r], d_sib)

    def rs(s, h):
        return remote(sbuf.at[s, h], rbuf.at[s, h], rss.at[s, h], rsr.at[s, h], d_y)

    def dm(k, p, h):
        return remote(dsb.at[k, p, h], drb.at[k, p, h], dms.at[k, p, h], dmr.at[k, p, h], d_end)

    def yf(k, h):
        return remote(drb.at[k, 1 - g, h], yrb.at[k, h], yfs.at[k, h], yfr.at[k, h], d_y)

    def project(j):
        r = order(z, j)

        @pl.loop(0, r + 1)
        def _(kc):
            t_sib(r, kc).wait_recv()
            t_fwd(r, kc).wait_recv()

        rows = pl.ds(pl.multiple_of(W * r, W), W)
        for b in range(nb):
            acc[...] = jnp.zeros_like(acc)

            @pl.loop(0, r + 1)
            def _(kc):
                t = tbuf[kc, b, rows, :]
                th = t.astype(bf16)
                tl = (t - th.astype(f32)).astype(bf16)
                ks = pl.ds(pl.multiple_of(W * kc, W), W)
                ch = chi[b, ks, :]
                acc[...] += (jnp.dot(th, ch, preferred_element_type=f32)
                             + jnp.dot(th, clo[b, ks, :], preferred_element_type=f32)
                             + jnp.dot(tl, ch, preferred_element_type=f32))

            full = acc[...]
            colbuf[z, r, W * b:W * (b + 1), :] = full.astype(bf16)
            rowt[c, r, :, W * b:W * (b + 1)] = full.T.astype(bf16)

        pin(z, r).start()
        px(0, c, r).start()
        px(1, c, r).start()

    t_first(0)
    cload.wait()
    for b in range(nb):
        cc = cbuf[b]
        hi = cc.astype(bf16)
        chi[b] = hi
        clo[b] = (cc - hi.astype(f32)).astype(bf16)
    t_first(1)
    t_first(2)
    t_second(0)
    project(0)
    t_first(3)
    t_second(1)
    project(1)
    t_second(2)
    project(2)
    t_second(3)
    project(3)

    def block(lhs, cp, s, lo, n):
        total = jnp.dot(lhs[cp, 0], colbuf[s, 0, :, lo:lo + n], preferred_element_type=f32)
        for rg in range(1, 4):
            total += jnp.dot(lhs[cp, rg], colbuf[s, rg, :, lo:lo + n], preferred_element_type=f32)
        return total

    def emit(s, h):
        cols = pl.ds(pl.multiple_of(W * s + H * h, H), H)
        return pltpu.make_async_copy(obuf.at[:, cols], out.at[:, cols], osem.at[s, h])

    def gram(s, halves):
        lo, n = H * halves[0], H * len(halves)
        cols = pl.ds(pl.multiple_of(W * s + lo, H), n)

        @pl.loop(0, 2)
        def _(i):
            t = encode(block(rowt, 2 * (1 - g) + i, s, lo, n))
            for k, h in enumerate(halves):
                sbuf[s, h, pl.ds(pl.multiple_of(W * i, W), W), :] = t[:, H * k:H * (k + 1)]

        for h in halves:
            rs(s, h).start()

        @pl.loop(0, 2)
        def _(i):
            obuf[pl.ds(pl.multiple_of(W * i, W), W), cols] = block(rowt, 2 * g + i, s, lo, n)

    def finish(s):
        for h in (0, 1):
            cols = pl.ds(pl.multiple_of(W * s + H * h, H), H)
            rs(s, h).wait_recv()
            obuf[:, cols] = obuf[:, cols] + decode(rbuf[s, h])
            emit(s, h).start()

    def lend(k, s, p, halves):
        lo, n = H * halves[0], H * len(halves)

        @pl.loop(0, 2)
        def _(i):
            t = encode(block(rowe, 2 * p + i, s, lo, n))
            for q, h in enumerate(halves):
                dsb[k, p, h, pl.ds(pl.multiple_of(W * i, W), W), :] = t[:, H * q:H * (q + 1)]

        for h in halves:
            dm(k, p, h).start()

    def near_rows(i):
        r = order(z, i)
        px(0, c, r).wait_recv()
        px(2, xn, r).start()

    def all_rows():
        for r in range(4):
            px(1, sib, r).wait_recv()
            px(2, xs, r).wait_recv()

    @pl.when(is_mid)
    def _():
        for i in range(4):
            r = order(e, i)
            pin(e, r).wait_recv()
            pfwd(e, r, 0).start()
            for b in range(nb):
                rowe[c, r, :, W * b:W * (b + 1)] = colbuf[e, r, W * b:W * (b + 1), :].astype(f32).T.astype(bf16)
            rshare(0, c, r).start()
        for i in range(4):
            pfwd(e, order(e, i), 1).start()
        for r in range(4):
            rshare(0, sib, r).wait_recv()
        lend(0, z, xp, (0, 1))
        for i in range(4):
            near_rows(i)
        all_rows()
        gram(z, (0, 1))
        gram(e, (0, 1))
        for i in range(4):
            pin(o, order(o, i)).wait_recv()
        lend(1, o, xp, (0, 1))
        gram(o, (0, 1))
        for i in range(4):
            r = order(e, i)
            rup(r).wait_recv()
            rshare(1, xn, r).start()
        for r in range(4):
            rshare(1, xs, r).wait_recv()
        lend(0, z, 1 - xp, (0, 1))
        lend(1, o, 1 - xp, (0, 1))
        finish(z)
        finish(e)
        for h in (0, 1):
            for i in range(4):
                pfwd(f, order(f, i), h).wait_recv()
            lend(2, f, 1 - g, (h,))
            gram(f, (h,))
            lend(2, f, g, (h,))
            if h == 0:
                finish(o)
        finish(f)

    def pass_on(k, p, h):
        dm(k, p, h).wait_recv()

        @pl.when(p != g)
        def _():
            yf(k, h).start()

    def settle(k, s, h):
        cols = pl.ds(pl.multiple_of(W * s + H * h, H), H)
        yf(k, h).wait_recv()
        obuf[:, cols] = decode(drb[k, g, h]) + decode(yrb[k, h])
        emit(s, h).start()

    @pl.when(is_end)
    def _():
        for i in range(4):
            near_rows(i)
            rup(order(z, i)).start()
        all_rows()
        gram(z, (0, 1))
        inner = 1 + z // 3
        for k in (0, 1):
            for h in (0, 1):
                pass_on(k, xp, h)
        finish(z)
        for k in (0, 1):
            for h in (0, 1):
                pass_on(k, 1 - xp, h)
        for k, s in ((0, inner), (1, 3 - inner)):
            for h in (0, 1):
                settle(k, s, h)
        for h in (0, 1):
            pass_on(2, 1 - g, h)
            pass_on(2, g, h)
            settle(2, 3 - z, h)

    for r in range(4):
        for kc in range(r + 1):
            @pl.when((r <= z) & (z < 3))
            def _():
                t_up(r, kc).wait_send()

            @pl.when((r >= z) & (z > 0))
            def _():
                t_dn(r, kc).wait_send()

            t_xn(r, kc).wait_send()
            t_sib(r, kc).wait_send()
            t_fwd(r, kc).wait_send()
        pin(z, r).wait_send()
        px(0, c, r).wait_send()
        px(1, c, r).wait_send()
        px(2, xn, r).wait_send()
        for h in (0, 1):
            emit(r, h).wait()

    @pl.when(is_mid)
    def _():
        for r in range(4):
            rshare(0, c, r).wait_send()
            rshare(1, xn, r).wait_send()
            for h in (0, 1):
                pfwd(e, r, h).wait_send()
                rs(r, h).wait_send()
        for k in range(3):
            for h in (0, 1):
                dm(k, 0, h).wait_send()
                dm(k, 1, h).wait_send()

    @pl.when(is_end)
    def _():
        for r in range(4):
            rup(r).wait_send()
        for h in (0, 1):
            rs(z, h).wait_send()
            for k in range(3):
                yf(k, h).wait_send()


def single(nb, fac, piv, c_hbm, out, tbuf, cbuf, chi, clo, acc, colbuf, rowt, obuf,
           csem, tss, trs, pzs, pzr, phs, phr, pxs, pxr, osem):
    g, z, c = lax.axis_index("grp"), lax.axis_index("row"), lax.axis_index("col")
    sib = c + 1 - 2 * (c % 2)
    xn = (c + 2) % 4
    d_up, d_dn = (g, z + 1, c), (g, z - 1, c)
    d_xn, d_sib = (g, z, xn), (g, z, sib)
    piece = fac.shape[1]

    def order(zz, j):
        if j == 0:
            return zz
        if j == 1:
            return zz - 1 + 2 * ((3 - zz) // 3)
        if j == 2:
            return zz + 1 + (3 - zz) // 3 - 3 * (zz // 3)
        return 3 - 3 * (zz // 2)

    cload = pltpu.make_async_copy(c_hbm, cbuf, csem)
    cload.start()

    bar = pltpu.get_barrier_semaphore()

    def hello(dev):
        pl.semaphore_signal(bar, inc=1, device_id=dev, device_id_type=MESH)

    hello(d_xn)
    hello(d_sib)

    @pl.when(z < 3)
    def _():
        hello(d_up)

    @pl.when(z > 0)
    def _():
        hello(d_dn)

    for kc in range(4):
        @pl.when(kc <= z)
        def _():
            start = W * z + piece * c
            rows = start + lax.broadcasted_iota(jnp.int32, (piece, W), 0)
            cols = W * kc + lax.broadcasted_iota(jnp.int32, (piece, W), 1)
            for b in range(nb):
                diag = jnp.where(cols == rows, jnp.broadcast_to(piv[b:b + 1, :], (piece, W)), 0.0)
                tbuf[kc, b, pl.ds(pl.multiple_of(start, piece), piece), :] = jnp.where(
                    cols < rows, fac[b, :, W * kc:W * (kc + 1)], diag)

    pl.semaphore_wait(bar, 2 + (z + 3) // 4 + 1 - z // 3)

    def remote(ref, ss, rs, dev):
        return pltpu.make_async_remote_copy(
            src_ref=ref, dst_ref=ref, send_sem=ss, recv_sem=rs, device_id=dev, device_id_type=MESH)

    def tcopy(route, arrive, r, kc, col, dev):
        ref = tbuf.at[kc, :, pl.ds(pl.multiple_of(W * r + piece * col, piece), piece), :]
        return remote(ref, tss.at[route, r, kc], trs.at[arrive, r, kc], dev)

    def t_up(r, kc):
        return tcopy(0, 0, r, kc, c, d_up)

    def t_dn(r, kc):
        return tcopy(1, 0, r, kc, c, d_dn)

    def t_xn(r, kc):
        return tcopy(2, 1, r, kc, c, d_xn)

    def t_sib(r, kc):
        return tcopy(3, 2, r, kc, c, d_sib)

    def t_fwd(r, kc):
        return tcopy(4, 3, r, kc, xn, d_sib)

    def t_first(j):
        r = order(z, j)

        @pl.loop(0, r + 1)
        def _(kc):
            if j > 0:
                t_up(r, kc).wait_recv()

            @pl.when((r <= z) & (z < 3))
            def _():
                t_up(r, kc).start()

            @pl.when((r >= z) & (z > 0))
            def _():
                t_dn(r, kc).start()

            t_xn(r, kc).start()
            t_sib(r, kc).start()

    def t_second(j):
        r = order(z, j)

        @pl.loop(0, r + 1)
        def _(kc):
            t_xn(r, kc).wait_recv()
            t_fwd(r, kc).start()

    def pz(s, rg, up):
        return remote(colbuf.at[s, rg], pzs.at[0 if up else 1, s, rg], pzr.at[s, rg], d_up if up else d_dn)

    def px(route, col, rg):
        return remote(rowt.at[col, rg], pxs.at[route, rg], pxr.at[route, rg], d_xn if route == 0 else d_sib)

    def project(j):
        r = order(z, j)

        @pl.loop(0, r + 1)
        def _(kc):
            t_sib(r, kc).wait_recv()
            t_fwd(r, kc).wait_recv()

        rows = pl.ds(pl.multiple_of(W * r, W), W)
        for b in range(nb):
            acc[...] = jnp.zeros_like(acc)

            @pl.loop(0, r + 1)
            def _(kc):
                t = tbuf[kc, b, rows, :]
                th = t.astype(bf16)
                tl = (t - th.astype(f32)).astype(bf16)
                ks = pl.ds(pl.multiple_of(W * kc, W), W)
                ch = chi[b, ks, :]
                acc[...] += (jnp.dot(th, ch, preferred_element_type=f32)
                             + jnp.dot(th, clo[b, ks, :], preferred_element_type=f32)
                             + jnp.dot(tl, ch, preferred_element_type=f32))

            full = acc[...]
            colbuf[z, r, W * b:W * (b + 1), :] = full.astype(bf16)
            rowt[c, r, :, W * b:W * (b + 1)] = full.T.astype(bf16)

        @pl.when(z < 3)
        def _():
            pz(z, r, True).start()

        @pl.when(z > 0)
        def _():
            pz(z, r, False).start()

        px(0, c, r).start()
        px(1, c, r).start()

    t_first(0)
    cload.wait()
    for b in range(nb):
        cc = cbuf[b]
        hi = cc.astype(bf16)
        chi[b] = hi
        clo[b] = (cc - hi.astype(f32)).astype(bf16)
    t_first(1)
    t_first(2)
    t_second(0)
    project(0)
    t_first(3)
    t_second(1)
    project(1)
    t_second(2)
    project(2)
    t_second(3)
    project(3)

    H = W // 2

    def block(cp, s, lo, n):
        total = jnp.dot(rowt[cp, 0], colbuf[s, 0, :, lo:lo + n], preferred_element_type=f32)
        for rg in range(1, 4):
            total += jnp.dot(rowt[cp, rg], colbuf[s, rg, :, lo:lo + n], preferred_element_type=f32)
        return total

    def emit(s, h):
        cols = pl.ds(pl.multiple_of(W * s + H * h, H), H)
        return pltpu.make_async_copy(obuf.at[:, cols], out.at[:, cols], osem.at[s, h])

    def gram(s, halves):
        lo, n = H * halves[0], H * len(halves)
        cols = pl.ds(pl.multiple_of(W * s + lo, H), n)
        @pl.loop(0, 4)
        def _(i):
            obuf[pl.ds(pl.multiple_of(W * i, W), W), cols] = block(i, s, lo, n)

    def finish(s):
        for h in (0, 1):
            emit(s, h).start()

    def ph(s, rg, h, up):
        return remote(colbuf.at[s, rg, :, H * h:H * (h + 1)], phs.at[rg, h], phr.at[rg, h], d_up if up else d_dn)

    def near(i):
        lo, hi = z - 1, z + 1

        @pl.when(lo >= 0)
        def _():
            rg = order(lo, i)
            pz(lo, rg, True).wait_recv()

            @pl.when(z < 3)
            def _():
                pz(lo, rg, True).start()

        @pl.when(hi <= 3)
        def _():
            rg = order(hi, i)
            pz(hi, rg, False).wait_recv()

            @pl.when(z > 0)
            def _():
                pz(hi, rg, False).start()

    def second(s, up):
        for i in range(4):
            pz(s, order(s, i), up).wait_recv()

        @pl.when((z == 1) | (z == 2))
        def _():
            for h in (0, 1):
                for rg in range(4):
                    ph(s, rg, h, up).start()

        gram(s, (0, 1))

    def third(s, up):
        for h in (0, 1):
            for rg in range(4):
                ph(s, rg, h, up).wait_recv()
            gram(s, (h,))

    def each(d, fn):
        @pl.when(z - d >= 0)
        def _():
            fn(z - d, True)

        @pl.when(z + d <= 3)
        def _():
            fn(z + d, False)

    for i in range(4):
        near(i)
        r = order(z, i)
        px(0, c, r).wait_recv()
        px(2, xn, r).start()
    for i in range(4):
        px(1, c, i).wait_recv()
        px(2, c, i).wait_recv()
    gram(z, (0, 1))
    each(1, lambda s, up: gram(s, (0, 1)))
    each(2, second)
    finish(z)
    each(1, lambda s, up: finish(s))
    each(3, third)
    each(2, lambda s, up: finish(s))
    each(3, lambda s, up: finish(s))

    for r in range(4):
        for kc in range(r + 1):
            @pl.when((r <= z) & (z < 3))
            def _():
                t_up(r, kc).wait_send()

            @pl.when((r >= z) & (z > 0))
            def _():
                t_dn(r, kc).wait_send()

            t_xn(r, kc).wait_send()
            t_sib(r, kc).wait_send()
            t_fwd(r, kc).wait_send()
        for s in range(4):
            @pl.when((s <= z) & (z < 3) & (z - s < 2))
            def _():
                pz(s, r, True).wait_send()

            @pl.when((s >= z) & (z > 0) & (s - z < 2))
            def _():
                pz(s, r, False).wait_send()

        px(0, c, r).wait_send()
        px(1, c, r).wait_send()
        px(2, xn, r).wait_send()
        for h in (0, 1):
            @pl.when((z == 1) | (z == 2))
            def _():
                ph(3, r, h, False).wait_send()

            emit(r, h).wait()


def body(groups, factor, pivots, constraints):
    nb, piece, order_m = factor.shape
    strip = constraints.shape[2]
    assert strip == W and order_m == 4 * W and piece * 4 == W
    dma = pltpu.SemaphoreType.DMA
    common = [
        pltpu.VMEM((4, nb, 4 * W, W), f32),
        pltpu.VMEM((nb, 4 * W, W), f32),
        pltpu.VMEM((nb, 4 * W, W), bf16),
        pltpu.VMEM((nb, 4 * W, W), bf16),
        pltpu.VMEM((W, W), f32),
        pltpu.VMEM((4, 4, nb * W, W), bf16),
        pltpu.VMEM((4, 4, W, nb * W), bf16),
    ]
    if groups == 2:
        kernel, rows_out = paired, 2 * W
        scratch = common + [
            pltpu.VMEM((4, 4, W, nb * W), bf16),
            pltpu.VMEM((rows_out, 4 * W), f32),
            pltpu.VMEM((4, 2, 2 * W, H), bf16),
            pltpu.VMEM((4, 2, 2 * W, H), bf16),
            pltpu.VMEM((3, 2, 2, 2 * W, H), bf16),
            pltpu.VMEM((3, 2, 2, 2 * W, H), bf16),
            pltpu.VMEM((3, 2, 2 * W, H), bf16),
            dma,
            dma((5, 4, 4)),
            dma((4, 4, 4)),
            dma((4,)),
            dma((4, 4)),
            dma((4, 2)),
            dma((4, 2)),
            dma((3, 4)),
            dma((3, 4)),
            dma((4,)),
            dma((4,)),
            dma((2, 4)),
            dma((2, 4)),
            dma((4, 2)),
            dma((4, 2)),
            dma((3, 2, 2)),
            dma((3, 2, 2)),
            dma((3, 2)),
            dma((3, 2)),
            dma((4, 2)),
        ]
    else:
        kernel, rows_out = single, 4 * W
        scratch = common + [
            pltpu.VMEM((rows_out, 4 * W), f32),
            dma,
            dma((5, 4, 4)),
            dma((4, 4, 4)),
            dma((2, 4, 4)),
            dma((4, 4)),
            dma((4, 2)),
            dma((4, 2)),
            dma((3, 4)),
            dma((3, 4)),
            dma((4, 2)),
        ]
    result = pl.pallas_call(
        functools.partial(kernel, nb),
        out_shape=jax.ShapeDtypeStruct((rows_out, 4 * W), f32),
        in_specs=[
            pl.BlockSpec(memory_space=pltpu.VMEM),
            pl.BlockSpec(memory_space=pltpu.VMEM),
            pl.BlockSpec(memory_space=pl.ANY),
        ],
        out_specs=pl.BlockSpec(memory_space=pl.ANY),
        scratch_shapes=scratch,
        compiler_params=pltpu.CompilerParams(
            collective_id=0, has_side_effects=True, vmem_limit_bytes=52 << 20),
    )(factor, jnp.tile(pivots, (1, 4)), constraints)
    if groups != 2:
        result = lax.psum_scatter(result, "grp", scatter_dimension=0, tiled=True)
    return result[None]


def solution(mesh):
    in_specs = (
        P("grp", ("row", "col"), None),
        P("grp", ("row", "col")),
        P("grp", None, ("col", "row")),
    )
    return jax.shard_map(
        functools.partial(body, mesh.shape["grp"]), mesh=mesh, in_specs=in_specs,
        out_specs=P("row", "grp", "col"), check_vma=False)
```

```python
import functools
import jax
import jax.numpy as jnp
from jax import lax
from jax.experimental import pallas as pl
from jax.experimental.pallas import tpu as pltpu
from jax.sharding import PartitionSpec as P

MESH = pl.DeviceIdType.MESH
f32 = jnp.float32
bf16 = jnp.bfloat16
W = 256


H = W // 2
GAIN = 8192.0


def encode(t):
    a = t * GAIN
    return (a * jnp.abs(a) * (a * a)).astype(bf16)


def decode(w):
    a = w.astype(f32)
    root = jnp.sqrt(jnp.sqrt(jnp.abs(a))) * (1.0 / GAIN)
    return jnp.where(a < 0, -root, root)


def order(zz, j):
    if j == 0:
        return zz
    if j == 1:
        return zz - 1 + 2 * ((3 - zz) // 3)
    if j == 2:
        return zz + 1 + (3 - zz) // 3 - 3 * (zz // 3)
    return 3 - 3 * (zz // 2)


def paired(nb, fac_hbm, piv_hbm, c_hbm, out, fac, piv, tbuf, cbuf, chi, clo, acc, colbuf, rowt, rowe, sbuf, rbuf,
           dsb, drb, yrb, csem, tss, trs, pis, pir, pos, por, pfs, pfr, pxs, pxr, res, rer, rcs, rcr, rss, rsr,
           dms, dmr, yfs, yfr):
    g, z, c = lax.axis_index("grp"), lax.axis_index("row"), lax.axis_index("col")
    sib = c + 1 - 2 * (c % 2)
    xn = (c + 2) % 4
    xs = (sib + 2) % 4
    xp = c // 2
    d_up, d_dn = (g, z + 1, c), (g, z - 1, c)
    d_xn, d_sib = (g, z, xn), (g, z, sib)
    d_y = (1 - g, z, c)
    e = 3 * (z // 2)
    f = 3 - e
    o = 3 - z
    d_in = (g, z + 1 - 2 * (z // 2), c)
    d_end = (g, e, c)
    is_mid = (z == 1) | (z == 2)
    is_end = (z == 0) | (z == 3)
    piece = fac.shape[1]

    fload = pltpu.make_async_copy(fac_hbm, fac, csem.at[0])
    pload = pltpu.make_async_copy(piv_hbm, piv, csem.at[1])
    cload = pltpu.make_async_copy(c_hbm, cbuf, csem.at[2])
    pload.start()
    fload.start()
    cload.start()

    bar = pltpu.get_barrier_semaphore()

    def hello(dev):
        pl.semaphore_signal(bar, inc=1, device_id=dev, device_id_type=MESH)

    hello(d_xn)
    hello(d_sib)
    hello(d_y)

    @pl.when(z < 3)
    def _():
        hello(d_up)

    @pl.when(z > 0)
    def _():
        hello(d_dn)

    pload.wait()
    fload.wait()
    for kc in range(4):
        @pl.when(kc <= z)
        def _():
            start = W * z + piece * c
            rows = start + lax.broadcasted_iota(jnp.int32, (piece, W), 0)
            cols = W * kc + lax.broadcasted_iota(jnp.int32, (piece, W), 1)
            for b in range(nb):
                own = jnp.concatenate([piv[b:b + 1, :]] * (W // piece), axis=1)
                diag = jnp.where(cols == rows, jnp.broadcast_to(own, (piece, W)), 0.0)
                tbuf[kc, b, pl.ds(pl.multiple_of(start, piece), piece), :] = jnp.where(
                    cols < rows, fac[b, :, W * kc:W * (kc + 1)], diag)

    pl.semaphore_wait(bar, 3 + (z + 3) // 4 + 1 - z // 3)

    def remote(src, dst, ss, rs, dev):
        return pltpu.make_async_remote_copy(
            src_ref=src, dst_ref=dst, send_sem=ss, recv_sem=rs, device_id=dev, device_id_type=MESH)

    def tcopy(route, arrive, r, kc, b, col, dev):
        ref = tbuf.at[kc, b, pl.ds(pl.multiple_of(W * r + piece * col, piece), piece), :]
        return remote(ref, ref, tss.at[route, r, kc, b], trs.at[arrive, r, kc, b], dev)

    def t_up(r, kc, b):
        return tcopy(0, 0, r, kc, b, c, d_up)

    def t_dn(r, kc, b):
        return tcopy(1, 0, r, kc, b, c, d_dn)

    def t_xn(r, kc, b):
        return tcopy(2, 1, r, kc, b, c, d_xn)

    def t_sib(r, kc, b):
        return tcopy(3, 2, r, kc, b, c, d_sib)

    def t_fwd(r, kc, b):
        return tcopy(4, 3, r, kc, b, xn, d_sib)

    def t_first(j, b):
        r = order(z, j)

        @pl.loop(0, r + 1)
        def _(kc):
            if j > 0:
                t_up(r, kc, b).wait_recv()

            @pl.when((r <= z) & (z < 3))
            def _():
                t_up(r, kc, b).start()

            @pl.when((r >= z) & (z > 0))
            def _():
                t_dn(r, kc, b).start()

            t_xn(r, kc, b).start()
            t_sib(r, kc, b).start()

    def t_second(j, b):
        r = order(z, j)

        @pl.loop(0, r + 1)
        def _(kc):
            t_xn(r, kc, b).wait_recv()
            t_fwd(r, kc, b).start()

    def pin(s, r, b):
        ref = colbuf.at[s, r, b]
        return remote(ref, ref, pis.at[r, b], pir.at[s, r, b], d_in)

    def pout(s, r, b):
        ref = colbuf.at[s, r, b]
        return remote(ref, ref, pos.at[r, b], por.at[r, b], d_end)

    def pfwd(s, r, b, h):
        ref = colbuf.at[s, r, b, :, H * h:H * (h + 1)]
        return remote(ref, ref, pfs.at[r, b, h], pfr.at[r, b, h], d_in)

    def px(route, col, r, b):
        ref = rowt.at[col, r, b]
        return remote(ref, ref, pxs.at[route, r, b], pxr.at[route, r, b], d_xn if route == 0 else d_sib)

    def rup(r, b):
        return remote(rowt.at[xn, r, b], rowe.at[xn, r, b], res.at[r, b], rer.at[r, b], d_in)

    def rshare(route, col, r, b):
        ref = rowe.at[col, r, b]
        return remote(ref, ref, rcs.at[route, r, b], rcr.at[route, r, b], d_sib)

    def rs(s, h):
        return remote(sbuf.at[s, h], rbuf.at[s, h], rss.at[s, h], rsr.at[s, h], d_y)

    def dm(k, p, h):
        return remote(dsb.at[k, p, h], drb.at[k, p, h], dms.at[k, p, h], dmr.at[k, p, h], d_end)

    def yf(k, h):
        return remote(drb.at[k, 1 - g, h], yrb.at[k, h], yfs.at[k, h], yfr.at[k, h], d_y)

    def project(j, b):
        r = order(z, j)
        rows = pl.ds(pl.multiple_of(W * r, W), W)

        @pl.loop(0, r + 1)
        def _(kc):
            t_sib(r, kc, b).wait_recv()
            t_fwd(r, kc, b).wait_recv()

        acc[...] = jnp.zeros_like(acc)

        @pl.loop(0, r + 1)
        def _(kc):
            t = tbuf[kc, b, rows, :]
            th = t.astype(bf16)
            tl = (t - th.astype(f32)).astype(bf16)
            ks = pl.ds(pl.multiple_of(W * kc, W), W)
            ch = chi[b, ks, :]
            acc[...] += (jnp.dot(th, ch, preferred_element_type=f32)
                         + jnp.dot(th, clo[b, ks, :], preferred_element_type=f32)
                         + jnp.dot(tl, ch, preferred_element_type=f32))

        full = acc[...]
        colbuf[z, r, b] = full.astype(bf16)
        pin(z, r, b).start()
        rowt[c, r, b] = full.T.astype(bf16)

    def split(b):
        cc = cbuf[b]
        hi = cc.astype(bf16)
        chi[b] = hi
        clo[b] = (cc - hi.astype(f32)).astype(bf16)

    def near(r, b):
        px(0, c, r, b).wait_recv()
        px(2, xn, r, b).start()

        @pl.when(is_end)
        def _():
            rup(r, b).start()

    def strip(r, b):
        pin(e, r, b).wait_recv()
        pfwd(e, r, b, 0).start()
        rowe[c, r, b] = colbuf[e, r, b].astype(f32).T.astype(bf16)
        rshare(0, c, r, b).start()

    def both(fn, zz, i):
        r = order(zz, i)
        for b in range(nb):
            fn(r, b)

    def first(j):
        for b in range(nb):
            t_first(j, b)

    def get(j):
        for b in range(nb):
            t_second(j, b)
            project(j, b)

    def across(r, b):
        px(0, c, r, b).start()
        px(1, c, r, b).start()

        @pl.when(is_mid)
        def _():
            pout(z, r, b).start()

    first(0)
    cload.wait()
    first(1)
    for b in range(nb):
        split(b)
    first(2)
    get(0)
    get(1)
    first(3)
    both(across, z, 0)
    both(across, z, 1)
    get(2)
    both(across, z, 2)
    get(3)
    both(across, z, 3)

    def block(lhs, cp, s, lo, n):
        total = jnp.dot(lhs[cp, 0, 0], colbuf[s, 0, 0, :, lo:lo + n], preferred_element_type=f32)
        for k in range(1, 4 * nb):
            total += jnp.dot(lhs[cp, k // nb, k % nb], colbuf[s, k // nb, k % nb, :, lo:lo + n],
                             preferred_element_type=f32)
        return total

    def send(s, halves):
        lo, n = H * halves[0], H * len(halves)

        @pl.loop(0, 2)
        def _(i):
            t = encode(block(rowt, 2 * (1 - g) + i, s, lo, n))
            for k, h in enumerate(halves):
                sbuf[s, h, pl.ds(pl.multiple_of(W * i, W), W), :] = t[:, H * k:H * (k + 1)]

        for h in halves:
            rs(s, h).start()

    def keep(s, halves):
        lo, n = H * halves[0], H * len(halves)
        cols = pl.ds(pl.multiple_of(W * s + lo, H), n)

        @pl.loop(0, 2)
        def _(i):
            out[pl.ds(pl.multiple_of(W * i, W), W), cols] = block(rowt, 2 * g + i, s, lo, n)

    def finish(s, h):
        cols = pl.ds(pl.multiple_of(W * s + H * h, H), H)
        rs(s, h).wait_recv()
        out[:, cols] = out[:, cols] + decode(rbuf[s, h])

    def lend(k, s, p, halves):
        lo, n = H * halves[0], H * len(halves)

        @pl.loop(0, 2)
        def _(i):
            t = encode(block(rowe, 2 * p + i, s, lo, n))
            for q, h in enumerate(halves):
                dsb[k, p, h, pl.ds(pl.multiple_of(W * i, W), W), :] = t[:, H * q:H * (q + 1)]

        for h in halves:
            dm(k, p, h).start()

    def every(fn):
        for r in range(4):
            for b in range(nb):
                fn(r, b)

    def all_rows(r, b):
        px(1, sib, r, b).wait_recv()
        px(2, xs, r, b).wait_recv()

    @pl.when(is_mid)
    def _():
        def turn(r, b):
            rup(r, b).wait_recv()
            rshare(1, xn, r, b).start()

        both(strip, e, 0)
        both(strip, e, 1)
        both(strip, e, 2)
        both(near, z, 0)
        both(strip, e, 3)
        for i in range(4):
            both(lambda r, b: pfwd(e, r, b, 1).start(), e, i)
        both(near, z, 1)
        for i in range(4):
            both(lambda r, b: pin(o, r, b).wait_recv(), o, i)
        every(lambda r, b: rshare(0, sib, r, b).wait_recv())
        lend(0, o, xp, (0, 1))
        both(near, z, 2)
        both(turn, e, 0)
        both(near, z, 3)
        every(all_rows)
        send(z, (0, 1))
        send(e, (0, 1))
        for i in range(4):
            both(lambda r, b: pfwd(f, r, b, 0).wait_recv(), f, i)
        lend(1, f, xp, (0,))
        send(o, (0, 1))
        for i in range(1, 4):
            both(turn, e, i)
        every(lambda r, b: rshare(1, xs, r, b).wait_recv())
        lend(0, o, 1 - xp, (0, 1))
        lend(1, f, 1 - xp, (0,))
        for i in range(4):
            both(lambda r, b: pfwd(f, r, b, 1).wait_recv(), f, i)
        lend(1, f, 1 - g, (1,))
        lend(1, f, g, (1,))
        send(f, (0, 1))
        keep(z, (0, 1))
        keep(e, (0, 1))
        keep(o, (0, 1))
        keep(f, (0, 1))
        for s in (z, e, o, f):
            finish(s, 0)
            finish(s, 1)

    def pass_on(k, p, h):
        dm(k, p, h).wait_recv()

        @pl.when(p != g)
        def _():
            yf(k, h).start()

    def settle(k, s, h):
        cols = pl.ds(pl.multiple_of(W * s + H * h, H), H)
        yf(k, h).wait_recv()
        out[:, cols] = decode(drb[k, g, h]) + decode(yrb[k, h])

    @pl.when(is_end)
    def _():
        inner = 1 + z // 3
        for i in range(4):
            both(near, z, i)
        every(all_rows)
        send(z, (0, 1))
        for i in range(4):
            both(lambda r, b: pout(inner, r, b).wait_recv(), inner, i)
        send(inner, (0, 1))
        pass_on(0, xp, 0)
        pass_on(0, xp, 1)
        pass_on(1, xp, 0)
        keep(z, (0, 1))
        keep(inner, (0, 1))
        for s in (z, inner):
            for h in (0, 1):
                finish(s, h)
        pass_on(0, 1 - xp, 0)
        pass_on(0, 1 - xp, 1)
        pass_on(1, 1 - xp, 0)
        settle(0, 3 - inner, 0)
        settle(0, 3 - inner, 1)
        settle(1, 3 - z, 0)
        pass_on(1, 1 - g, 1)
        pass_on(1, g, 1)
        settle(1, 3 - z, 1)

    def sent(r, b):
        for kc in range(4):
            @pl.when(kc <= r)
            def _():
                @pl.when((r <= z) & (z < 3))
                def _():
                    t_up(r, kc, b).wait_send()

                @pl.when((r >= z) & (z > 0))
                def _():
                    t_dn(r, kc, b).wait_send()

                t_xn(r, kc, b).wait_send()
                t_sib(r, kc, b).wait_send()
                t_fwd(r, kc, b).wait_send()
        pin(z, r, b).wait_send()
        px(0, c, r, b).wait_send()
        px(1, c, r, b).wait_send()
        px(2, xn, r, b).wait_send()

        @pl.when(is_mid)
        def _():
            pout(z, r, b).wait_send()
            rshare(0, c, r, b).wait_send()
            rshare(1, xn, r, b).wait_send()
            pfwd(e, r, b, 0).wait_send()
            pfwd(e, r, b, 1).wait_send()

        @pl.when(is_end)
        def _():
            rup(r, b).wait_send()

    @pl.loop(0, 4)
    def _(r):
        for b in range(nb):
            sent(r, b)

    for h in (0, 1):
        rs(z, h).wait_send()
        rs(z + 1 - 2 * (z // 2), h).wait_send()

        @pl.when(is_mid)
        def _():
            rs(e, h).wait_send()
            rs(f, h).wait_send()
            for k in (0, 1):
                dm(k, 0, h).wait_send()
                dm(k, 1, h).wait_send()

        @pl.when(is_end)
        def _():
            yf(0, h).wait_send()
            yf(1, h).wait_send()


def single(nb, fac, piv, c_hbm, out, tbuf, cbuf, chi, clo, acc, colbuf, rowt, obuf,
           csem, tss, trs, pzs, pzr, phs, phr, pxs, pxr, osem):
    g, z, c = lax.axis_index("grp"), lax.axis_index("row"), lax.axis_index("col")
    sib = c + 1 - 2 * (c % 2)
    xn = (c + 2) % 4
    d_up, d_dn = (g, z + 1, c), (g, z - 1, c)
    d_xn, d_sib = (g, z, xn), (g, z, sib)
    piece = fac.shape[1]

    def order(zz, j):
        if j == 0:
            return zz
        if j == 1:
            return zz - 1 + 2 * ((3 - zz) // 3)
        if j == 2:
            return zz + 1 + (3 - zz) // 3 - 3 * (zz // 3)
        return 3 - 3 * (zz // 2)

    cload = pltpu.make_async_copy(c_hbm, cbuf, csem)
    cload.start()

    bar = pltpu.get_barrier_semaphore()

    def hello(dev):
        pl.semaphore_signal(bar, inc=1, device_id=dev, device_id_type=MESH)

    hello(d_xn)
    hello(d_sib)

    @pl.when(z < 3)
    def _():
        hello(d_up)

    @pl.when(z > 0)
    def _():
        hello(d_dn)

    for kc in range(4):
        @pl.when(kc <= z)
        def _():
            start = W * z + piece * c
            rows = start + lax.broadcasted_iota(jnp.int32, (piece, W), 0)
            cols = W * kc + lax.broadcasted_iota(jnp.int32, (piece, W), 1)
            for b in range(nb):
                diag = jnp.where(cols == rows, jnp.broadcast_to(piv[b:b + 1, :], (piece, W)), 0.0)
                tbuf[kc, b, pl.ds(pl.multiple_of(start, piece), piece), :] = jnp.where(
                    cols < rows, fac[b, :, W * kc:W * (kc + 1)], diag)

    pl.semaphore_wait(bar, 2 + (z + 3) // 4 + 1 - z // 3)

    def remote(ref, ss, rs, dev):
        return pltpu.make_async_remote_copy(
            src_ref=ref, dst_ref=ref, send_sem=ss, recv_sem=rs, device_id=dev, device_id_type=MESH)

    def tcopy(route, arrive, r, kc, col, dev):
        ref = tbuf.at[kc, :, pl.ds(pl.multiple_of(W * r + piece * col, piece), piece), :]
        return remote(ref, tss.at[route, r, kc], trs.at[arrive, r, kc], dev)

    def t_up(r, kc):
        return tcopy(0, 0, r, kc, c, d_up)

    def t_dn(r, kc):
        return tcopy(1, 0, r, kc, c, d_dn)

    def t_xn(r, kc):
        return tcopy(2, 1, r, kc, c, d_xn)

    def t_sib(r, kc):
        return tcopy(3, 2, r, kc, c, d_sib)

    def t_fwd(r, kc):
        return tcopy(4, 3, r, kc, xn, d_sib)

    def t_first(j):
        r = order(z, j)

        @pl.loop(0, r + 1)
        def _(kc):
            if j > 0:
                t_up(r, kc).wait_recv()

            @pl.when((r <= z) & (z < 3))
            def _():
                t_up(r, kc).start()

            @pl.when((r >= z) & (z > 0))
            def _():
                t_dn(r, kc).start()

            t_xn(r, kc).start()
            t_sib(r, kc).start()

    def t_second(j):
        r = order(z, j)

        @pl.loop(0, r + 1)
        def _(kc):
            t_xn(r, kc).wait_recv()
            t_fwd(r, kc).start()

    def pz(s, rg, up):
        return remote(colbuf.at[s, rg], pzs.at[0 if up else 1, s, rg], pzr.at[s, rg], d_up if up else d_dn)

    def px(route, col, rg):
        return remote(rowt.at[col, rg], pxs.at[route, rg], pxr.at[route, rg], d_xn if route == 0 else d_sib)

    def project(j):
        r = order(z, j)

        @pl.loop(0, r + 1)
        def _(kc):
            t_sib(r, kc).wait_recv()
            t_fwd(r, kc).wait_recv()

        rows = pl.ds(pl.multiple_of(W * r, W), W)
        for b in range(nb):
            acc[...] = jnp.zeros_like(acc)

            @pl.loop(0, r + 1)
            def _(kc):
                t = tbuf[kc, b, rows, :]
                th = t.astype(bf16)
                tl = (t - th.astype(f32)).astype(bf16)
                ks = pl.ds(pl.multiple_of(W * kc, W), W)
                ch = chi[b, ks, :]
                acc[...] += (jnp.dot(th, ch, preferred_element_type=f32)
                             + jnp.dot(th, clo[b, ks, :], preferred_element_type=f32)
                             + jnp.dot(tl, ch, preferred_element_type=f32))

            full = acc[...]
            colbuf[z, r, W * b:W * (b + 1), :] = full.astype(bf16)
            rowt[c, r, :, W * b:W * (b + 1)] = full.T.astype(bf16)

        @pl.when(z < 3)
        def _():
            pz(z, r, True).start()

        @pl.when(z > 0)
        def _():
            pz(z, r, False).start()

        px(0, c, r).start()
        px(1, c, r).start()

    t_first(0)
    cload.wait()
    for b in range(nb):
        cc = cbuf[b]
        hi = cc.astype(bf16)
        chi[b] = hi
        clo[b] = (cc - hi.astype(f32)).astype(bf16)
    t_first(1)
    t_first(2)
    t_second(0)
    project(0)
    t_first(3)
    t_second(1)
    project(1)
    t_second(2)
    project(2)
    t_second(3)
    project(3)

    H = W // 2

    def block(cp, s, lo, n):
        total = jnp.dot(rowt[cp, 0], colbuf[s, 0, :, lo:lo + n], preferred_element_type=f32)
        for rg in range(1, 4):
            total += jnp.dot(rowt[cp, rg], colbuf[s, rg, :, lo:lo + n], preferred_element_type=f32)
        return total

    def emit(s, h):
        cols = pl.ds(pl.multiple_of(W * s + H * h, H), H)
        return pltpu.make_async_copy(obuf.at[:, cols], out.at[:, cols], osem.at[s, h])

    def gram(s, halves):
        lo, n = H * halves[0], H * len(halves)
        cols = pl.ds(pl.multiple_of(W * s + lo, H), n)
        @pl.loop(0, 4)
        def _(i):
            obuf[pl.ds(pl.multiple_of(W * i, W), W), cols] = block(i, s, lo, n)

    def finish(s):
        for h in (0, 1):
            emit(s, h).start()

    def ph(s, rg, h, up):
        return remote(colbuf.at[s, rg, :, H * h:H * (h + 1)], phs.at[rg, h], phr.at[rg, h], d_up if up else d_dn)

    def near(i):
        lo, hi = z - 1, z + 1

        @pl.when(lo >= 0)
        def _():
            rg = order(lo, i)
            pz(lo, rg, True).wait_recv()

            @pl.when(z < 3)
            def _():
                pz(lo, rg, True).start()

        @pl.when(hi <= 3)
        def _():
            rg = order(hi, i)
            pz(hi, rg, False).wait_recv()

            @pl.when(z > 0)
            def _():
                pz(hi, rg, False).start()

    def second(s, up):
        for i in range(4):
            pz(s, order(s, i), up).wait_recv()

        @pl.when((z == 1) | (z == 2))
        def _():
            for h in (0, 1):
                for rg in range(4):
                    ph(s, rg, h, up).start()

        gram(s, (0, 1))

    def third(s, up):
        for h in (0, 1):
            for rg in range(4):
                ph(s, rg, h, up).wait_recv()
            gram(s, (h,))

    def each(d, fn):
        @pl.when(z - d >= 0)
        def _():
            fn(z - d, True)

        @pl.when(z + d <= 3)
        def _():
            fn(z + d, False)

    for i in range(4):
        near(i)
        r = order(z, i)
        px(0, c, r).wait_recv()
        px(2, xn, r).start()
    for i in range(4):
        px(1, c, i).wait_recv()
        px(2, c, i).wait_recv()
    gram(z, (0, 1))
    each(1, lambda s, up: gram(s, (0, 1)))
    each(2, second)
    finish(z)
    each(1, lambda s, up: finish(s))
    each(3, third)
    each(2, lambda s, up: finish(s))
    each(3, lambda s, up: finish(s))

    for r in range(4):
        for kc in range(r + 1):
            @pl.when((r <= z) & (z < 3))
            def _():
                t_up(r, kc).wait_send()

            @pl.when((r >= z) & (z > 0))
            def _():
                t_dn(r, kc).wait_send()

            t_xn(r, kc).wait_send()
            t_sib(r, kc).wait_send()
            t_fwd(r, kc).wait_send()
        for s in range(4):
            @pl.when((s <= z) & (z < 3) & (z - s < 2))
            def _():
                pz(s, r, True).wait_send()

            @pl.when((s >= z) & (z > 0) & (s - z < 2))
            def _():
                pz(s, r, False).wait_send()

        px(0, c, r).wait_send()
        px(1, c, r).wait_send()
        px(2, xn, r).wait_send()
        for h in (0, 1):
            @pl.when((z == 1) | (z == 2))
            def _():
                ph(3, r, h, False).wait_send()

            emit(r, h).wait()


LIMIT = 50


def body(groups, factor, pivots, constraints):
    nb, piece, order_m = factor.shape
    strip = constraints.shape[2]
    assert strip == W and order_m == 4 * W and piece * 4 == W
    dma = pltpu.SemaphoreType.DMA
    wide = [
        pltpu.VMEM((4, nb, 4 * W, W), f32),
        pltpu.VMEM((nb, 4 * W, W), f32),
        pltpu.VMEM((nb, 4 * W, W), bf16),
        pltpu.VMEM((nb, 4 * W, W), bf16),
        pltpu.VMEM((W, W), f32),
    ]
    vmem, anywhere = pl.BlockSpec(memory_space=pltpu.VMEM), pl.BlockSpec(memory_space=pl.ANY)
    if groups == 2:
        kernel, rows_out, limit = paired, 2 * W, LIMIT
        in_specs, out_specs = [anywhere] * 3, vmem
        scratch = [pltpu.VMEM((nb, piece, 4 * W), f32), pltpu.VMEM((nb, piece), f32)] + wide + [
            pltpu.VMEM((4, 4, nb, W, W), bf16),
            pltpu.VMEM((4, 4, nb, W, W), bf16),
            pltpu.VMEM((4, 4, nb, W, W), bf16),
            pltpu.VMEM((4, 2, 2 * W, H), bf16),
            pltpu.VMEM((4, 2, 2 * W, H), bf16),
            pltpu.VMEM((2, 2, 2, 2 * W, H), bf16),
            pltpu.VMEM((2, 2, 2, 2 * W, H), bf16),
            pltpu.VMEM((2, 2, 2 * W, H), bf16),
            dma((3,)),
            dma((5, 4, 4, nb)),
            dma((4, 4, 4, nb)),
            dma((4, nb)),
            dma((4, 4, nb)),
            dma((4, nb)),
            dma((4, nb)),
            dma((4, nb, 2)),
            dma((4, nb, 2)),
            dma((3, 4, nb)),
            dma((3, 4, nb)),
            dma((4, nb)),
            dma((4, nb)),
            dma((2, 4, nb)),
            dma((2, 4, nb)),
            dma((4, 2)),
            dma((4, 2)),
            dma((2, 2, 2)),
            dma((2, 2, 2)),
            dma((2, 2)),
            dma((2, 2)),
        ]
    else:
        kernel, rows_out, limit = single, 4 * W, 52
        pivots = jnp.tile(pivots, (1, 4))
        in_specs, out_specs = [vmem, vmem, anywhere], anywhere
        scratch = wide + [
            pltpu.VMEM((4, 4, nb * W, W), bf16),
            pltpu.VMEM((4, 4, W, nb * W), bf16),
            pltpu.VMEM((rows_out, 4 * W), f32),
            dma,
            dma((5, 4, 4)),
            dma((4, 4, 4)),
            dma((2, 4, 4)),
            dma((4, 4)),
            dma((4, 2)),
            dma((4, 2)),
            dma((3, 4)),
            dma((3, 4)),
            dma((4, 2)),
        ]
    result = pl.pallas_call(
        functools.partial(kernel, nb),
        out_shape=jax.ShapeDtypeStruct((rows_out, 4 * W), f32),
        in_specs=in_specs,
        out_specs=out_specs,
        scratch_shapes=scratch,
        compiler_params=pltpu.CompilerParams(
            collective_id=0, has_side_effects=True, vmem_limit_bytes=limit << 20),
    )(factor, pivots, constraints)
    if groups != 2:
        result = lax.psum_scatter(result, "grp", scatter_dimension=0, tiled=True)
    return result[None]


def solution(mesh):
    in_specs = (
        P("grp", ("row", "col"), None),
        P("grp", ("row", "col")),
        P("grp", None, ("col", "row")),
    )
    return jax.shard_map(
        functools.partial(body, mesh.shape["grp"]), mesh=mesh, in_specs=in_specs,
        out_specs=P("row", "grp", "col"), check_vma=False)
```

```python
import functools
import jax
import jax.numpy as jnp
from jax import lax
from jax.experimental import pallas as pl
from jax.experimental.pallas import tpu as pltpu
from jax.sharding import PartitionSpec as P

MESH = pl.DeviceIdType.MESH
f32 = jnp.float32
bf16 = jnp.bfloat16
W = 256


H = W // 2
GAIN = 8192.0


def encode(t):
    a = t * GAIN
    return (a * jnp.abs(a) * (a * a)).astype(bf16)


def decode(w):
    a = w.astype(f32)
    root = jnp.sqrt(jnp.sqrt(jnp.abs(a))) * (1.0 / GAIN)
    return jnp.where(a < 0, -root, root)


def order(zz, j):
    if j == 0:
        return zz
    if j == 1:
        return zz - 1 + 2 * ((3 - zz) // 3)
    if j == 2:
        return zz + 1 + (3 - zz) // 3 - 3 * (zz // 3)
    return 3 - 3 * (zz // 2)


def paired(nb, fac_hbm, piv_hbm, c_hbm, out, fac, piv, tbuf, cbuf, chi, clo, acc, colbuf, rowt, rowe, sbuf, rbuf,
           dsb, drb, yrb, csem, tss, trs, pis, pir, pos, por, pfs, pfr, pxs, pxr, res, rer, rcs, rcr, rss, rsr,
           dms, dmr, yfs, yfr):
    g, z, c = lax.axis_index("grp"), lax.axis_index("row"), lax.axis_index("col")
    sib = c + 1 - 2 * (c % 2)
    xn = (c + 2) % 4
    xs = (sib + 2) % 4
    xp = c // 2
    d_up, d_dn = (g, z + 1, c), (g, z - 1, c)
    d_xn, d_sib = (g, z, xn), (g, z, sib)
    d_y = (1 - g, z, c)
    e = 3 * (z // 2)
    f = 3 - e
    o = 3 - z
    d_in = (g, z + 1 - 2 * (z // 2), c)
    d_end = (g, e, c)
    is_mid = (z == 1) | (z == 2)
    is_end = (z == 0) | (z == 3)
    piece = fac.shape[1]

    fload = pltpu.make_async_copy(fac_hbm, fac, csem.at[0])
    pload = pltpu.make_async_copy(piv_hbm, piv, csem.at[1])
    cload = pltpu.make_async_copy(c_hbm, cbuf, csem.at[2])
    pload.start()
    fload.start()
    cload.start()

    bar = pltpu.get_barrier_semaphore()

    def hello(dev):
        pl.semaphore_signal(bar, inc=1, device_id=dev, device_id_type=MESH)

    hello(d_xn)
    hello(d_sib)
    hello(d_y)

    @pl.when(z < 3)
    def _():
        hello(d_up)

    @pl.when(z > 0)
    def _():
        hello(d_dn)

    pload.wait()
    fload.wait()
    for kc in range(4):
        @pl.when(kc <= z)
        def _():
            start = W * z + piece * c
            rows = start + lax.broadcasted_iota(jnp.int32, (piece, W), 0)
            cols = W * kc + lax.broadcasted_iota(jnp.int32, (piece, W), 1)
            for b in range(nb):
                own = jnp.concatenate([piv[b:b + 1, :]] * (W // piece), axis=1)
                diag = jnp.where(cols == rows, jnp.broadcast_to(own, (piece, W)), 0.0)
                tbuf[kc, b, pl.ds(pl.multiple_of(start, piece), piece), :] = jnp.where(
                    cols < rows, fac[b, :, W * kc:W * (kc + 1)], diag)

    pl.semaphore_wait(bar, 3 + (z + 3) // 4 + 1 - z // 3)

    def remote(src, dst, ss, rs, dev):
        return pltpu.make_async_remote_copy(
            src_ref=src, dst_ref=dst, send_sem=ss, recv_sem=rs, device_id=dev, device_id_type=MESH)

    def tcopy(route, arrive, r, kc, b, col, dev):
        ref = tbuf.at[kc, b, pl.ds(pl.multiple_of(W * r + piece * col, piece), piece), :]
        return remote(ref, ref, tss.at[route, r, kc, b], trs.at[arrive, r, kc, b], dev)

    def t_up(r, kc, b):
        return tcopy(0, 0, r, kc, b, c, d_up)

    def t_dn(r, kc, b):
        return tcopy(1, 0, r, kc, b, c, d_dn)

    def t_xn(r, kc, b):
        return tcopy(2, 1, r, kc, b, c, d_xn)

    def t_sib(r, kc, b):
        return tcopy(3, 2, r, kc, b, c, d_sib)

    def t_fwd(r, kc, b):
        return tcopy(4, 3, r, kc, b, xn, d_sib)

    def t_first(j, b):
        r = order(z, j)

        @pl.loop(0, r + 1)
        def _(kc):
            if j > 0:
                t_up(r, kc, b).wait_recv()

            @pl.when((r <= z) & (z < 3))
            def _():
                t_up(r, kc, b).start()

            @pl.when((r >= z) & (z > 0))
            def _():
                t_dn(r, kc, b).start()

            t_xn(r, kc, b).start()
            t_sib(r, kc, b).start()

    def t_second(j, b):
        r = order(z, j)

        @pl.loop(0, r + 1)
        def _(kc):
            t_xn(r, kc, b).wait_recv()
            t_fwd(r, kc, b).start()

    def pin(s, r, b):
        ref = colbuf.at[s, r, b]
        return remote(ref, ref, pis.at[r, b], pir.at[s, r, b], d_in)

    def pout(s, r, b):
        ref = colbuf.at[s, r, b]
        return remote(ref, ref, pos.at[r, b], por.at[r, b], d_end)

    def pfwd(s, r, b, h):
        ref = colbuf.at[s, r, b, :, H * h:H * (h + 1)]
        return remote(ref, ref, pfs.at[r, b, h], pfr.at[r, b, h], d_in)

    def px(route, col, r, b, m):
        ref = rowt.at[col, r, b, H * m:H * (m + 1), :]
        return remote(ref, ref, pxs.at[route, r, b, m], pxr.at[route, r, b, m], d_xn if route == 0 else d_sib)

    def rup(r, b, m):
        part = (xn, r, b, slice(H * m, H * (m + 1)), slice(None))
        return remote(rowt.at[part], rowe.at[part], res.at[r, b, m], rer.at[r, b, m], d_in)

    def rshare(route, col, r, b, m):
        ref = rowe.at[col, r, b, H * m:H * (m + 1), :]
        return remote(ref, ref, rcs.at[route, r, b, m], rcr.at[route, r, b, m], d_sib)

    def rs(s, h, m):
        return remote(sbuf.at[s, h, m], rbuf.at[s, h, m], rss.at[s, h, m], rsr.at[s, h, m], d_y)

    def dm(k, p, h, m):
        return remote(dsb.at[k, p, h, m], drb.at[k, p, h, m], dms.at[k, p, h, m], dmr.at[k, p, h, m], d_end)

    def yf(k, h, m):
        return remote(drb.at[k, 1 - g, h, m], yrb.at[k, h, m], yfs.at[k, h, m], yfr.at[k, h, m], d_y)

    def project(j, b):
        r = order(z, j)
        rows = pl.ds(pl.multiple_of(W * r, W), W)

        @pl.loop(0, r + 1)
        def _(kc):
            t_sib(r, kc, b).wait_recv()
            t_fwd(r, kc, b).wait_recv()

        acc[...] = jnp.zeros_like(acc)

        @pl.loop(0, r + 1)
        def _(kc):
            t = tbuf[kc, b, rows, :]
            th = t.astype(bf16)
            tl = (t - th.astype(f32)).astype(bf16)
            ks = pl.ds(pl.multiple_of(W * kc, W), W)
            ch = chi[b, ks, :]
            acc[...] += (jnp.dot(th, ch, preferred_element_type=f32)
                         + jnp.dot(th, clo[b, ks, :], preferred_element_type=f32)
                         + jnp.dot(tl, ch, preferred_element_type=f32))

        full = acc[...]
        colbuf[z, r, b] = full.astype(bf16)
        pin(z, r, b).start()
        rowt[c, r, b] = full.T.astype(bf16)

    def split(b):
        cc = cbuf[b]
        hi = cc.astype(bf16)
        chi[b] = hi
        clo[b] = (cc - hi.astype(f32)).astype(bf16)

    def near(m):
        def fn(r, b):
            px(0, c, r, b, m).wait_recv()
            px(2, xn, r, b, m).start()

            @pl.when(is_end)
            def _():
                rup(r, b, m).start()
        return fn

    def strip(r, b):
        pin(e, r, b).wait_recv()
        pfwd(e, r, b, 0).start()
        rowe[c, r, b] = colbuf[e, r, b].astype(f32).T.astype(bf16)
        rshare(0, c, r, b, 0).start()
        rshare(0, c, r, b, 1).start()

    def both(fn, zz, i):
        r = order(zz, i)
        for b in range(nb):
            fn(r, b)

    def first(j):
        for b in range(nb):
            t_first(j, b)

    def get(j):
        for b in range(nb):
            t_second(j, b)
            project(j, b)

    def across(m):
        def fn(r, b):
            px(0, c, r, b, m).start()
            px(1, c, r, b, m).start()
        return fn

    def outward(r, b):
        @pl.when(is_mid)
        def _():
            pout(z, r, b).start()

    first(0)
    cload.wait()
    t_first(1, 0)
    split(0)
    t_first(1, 1)
    split(1)

    @pl.when(is_end)
    def _():
        get(0)

    first(2)

    @pl.when(is_mid)
    def _():
        get(0)

    get(1)
    first(3)
    get(2)
    for i in range(3):
        both(across(0), z, i)
    get(3)
    both(across(0), z, 3)
    for i in range(4):
        both(outward, z, i)
        both(across(1), z, i)

    def block(lhs, cp, ro, rn, s, lo, n):
        total = jnp.dot(lhs[cp, 0, 0, ro:ro + rn, :], colbuf[s, 0, 0, :, lo:lo + n], preferred_element_type=f32)
        for k in range(1, 4 * nb):
            total += jnp.dot(lhs[cp, k // nb, k % nb, ro:ro + rn, :], colbuf[s, k // nb, k % nb, :, lo:lo + n],
                             preferred_element_type=f32)
        return total

    both_halves = (0, 1)

    def coded(lhs, p, s, halves, ms, ref, at):
        lo, n, ro, rn = H * halves[0], H * len(halves), H * ms[0], H * len(ms)

        @pl.loop(0, 2)
        def _(i):
            t = encode(block(lhs, 2 * p + i, ro, rn, s, lo, n))
            for q, h in enumerate(halves):
                for u, m in enumerate(ms):
                    ref[(*at, h, m, pl.ds(pl.multiple_of(H * i, H), H), slice(None))] = (
                        t[H * u:H * (u + 1), H * q:H * (q + 1)])

    def send(s, halves, ms):
        coded(rowt, 1 - g, s, halves, ms, sbuf, (s,))
        for h in halves:
            for m in ms:
                rs(s, h, m).start()

    def lend(k, s, p, halves, ms):
        coded(rowe, p, s, halves, ms, dsb, (k, p))
        for h in halves:
            for m in ms:
                dm(k, p, h, m).start()

    def keep(s, ms):
        cols, ro, rn = pl.ds(pl.multiple_of(W * s, W), W), H * ms[0], H * len(ms)

        @pl.loop(0, 2)
        def _(i):
            out[pl.ds(pl.multiple_of(W * i + ro, H), rn), cols] = block(rowt, 2 * g + i, ro, rn, s, 0, W)

    def work(s, p, ms):
        @pl.when(p == g)
        def _():
            keep(s, ms)

        @pl.when(p != g)
        def _():
            send(s, both_halves, ms)

    def parts(s):
        for h in (0, 1):
            cols = pl.ds(pl.multiple_of(W * s + H * h, H), H)
            for m in (0, 1):
                for i in (0, 1):
                    yield h, m, i, slice(W * i + H * m, W * i + H * (m + 1)), cols, slice(H * i, H * (i + 1))

    def finish(s):
        for h, m, i, rows, cols, part in parts(s):
            if i == 0:
                rs(s, h, m).wait_recv()
            out[rows, cols] = out[rows, cols] + decode(rbuf[s, h, m, part, :])

    def settle(k, s, hs):
        for h, m, i, rows, cols, part in parts(s):
            if h in hs:
                if i == 0:
                    yf(k, h, m).wait_recv()
                out[rows, cols] = decode(drb[k, g, h, m, part, :]) + decode(yrb[k, h, m, part, :])

    def pass_on(k, p, h, m):
        dm(k, p, h, m).wait_recv()

        @pl.when(p != g)
        def _():
            yf(k, h, m).start()

    def every(fn):
        for r in range(4):
            for b in range(nb):
                fn(r, b)

    def sib_rows():
        for m in (0, 1):
            every(lambda r, b: px(1, sib, r, b, m).wait_recv())

    def far_rows(m):
        every(lambda r, b: px(2, xs, r, b, m).wait_recv())

    def lent_rows(route, col, ms):
        for m in ms:
            every(lambda r, b: rshare(route, col, r, b, m).wait_recv())

    @pl.when(is_mid)
    def _():
        def turn(m):
            def fn(r, b):
                rup(r, b, m).wait_recv()
                rshare(1, xn, r, b, m).start()
            return fn

        both(strip, e, 0)
        both(strip, e, 1)
        sib_rows()
        work(z, xp, both_halves)
        both(near(0), z, 0)
        both(near(0), z, 1)
        both(strip, e, 2)
        both(near(0), z, 2)
        both(strip, e, 3)
        for i in range(4):
            both(lambda r, b: pfwd(e, r, b, 1).start(), e, i)
        both(near(0), z, 3)
        work(e, xp, both_halves)
        far_rows(0)
        work(z, 1 - xp, (0,))
        work(e, 1 - xp, (0,))
        for i in range(4):
            both(lambda r, b: pin(o, r, b).wait_recv(), o, i)
        lent_rows(0, sib, both_halves)
        lend(0, o, xp, both_halves, both_halves)
        both(near(1), z, 0)
        both(near(1), z, 1)
        work(o, 1 - xp, (0,))
        for i in range(4):
            if i >= 2:
                both(near(1), z, i)
            both(turn(0), e, i)
        far_rows(1)
        for s in (z, e, o):
            work(s, 1 - xp, (1,))
        lent_rows(1, xs, (0,))
        lend(0, o, 1 - xp, both_halves, (0,))
        for i in range(4):
            both(lambda r, b: pfwd(f, r, b, 0).wait_recv(), f, i)
        lend(1, f, xp, (0,), both_halves)
        lend(1, f, 1 - xp, (0,), (0,))
        work(o, xp, both_halves)
        for i in range(4):
            both(turn(1), e, i)
        lent_rows(1, xs, (1,))
        lend(0, o, 1 - xp, both_halves, (1,))
        lend(1, f, 1 - xp, (0,), (1,))
        for i in range(4):
            both(lambda r, b: pfwd(f, r, b, 1).wait_recv(), f, i)
        lend(1, f, 1 - g, (1,), both_halves)
        lend(1, f, g, (1,), both_halves)
        send(f, both_halves, both_halves)
        keep(f, both_halves)
        for s in (z, e, o, f):
            finish(s)

    @pl.when(is_end)
    def _():
        inner = 1 + z // 3
        both(near(0), z, 0)
        sib_rows()
        work(z, xp, both_halves)
        for i in range(1, 4):
            both(near(0), z, i)
        far_rows(0)
        work(z, 1 - xp, (0,))
        both(near(1), z, 0)
        both(near(1), z, 1)
        for i in range(4):
            both(lambda r, b: pout(inner, r, b).wait_recv(), inner, i)
        work(inner, 1 - xp, (0,))
        both(near(1), z, 2)
        both(near(1), z, 3)
        far_rows(1)
        work(z, 1 - xp, (1,))
        work(inner, 1 - xp, (1,))
        work(inner, xp, both_halves)

        def pass_both(k, p, hs, ms):
            for h in hs:
                for m in ms:
                    pass_on(k, p, h, m)

        pass_both(0, xp, both_halves, both_halves)
        pass_both(0, 1 - xp, both_halves, (0,))
        pass_both(1, xp, (0,), both_halves)
        pass_both(1, 1 - xp, (0,), (0,))
        finish(z)
        finish(inner)
        pass_both(0, 1 - xp, both_halves, (1,))
        pass_both(1, 1 - xp, (0,), (1,))
        settle(0, 3 - inner, both_halves)
        pass_both(1, 1 - g, (1,), both_halves)
        settle(1, 3 - z, (0,))
        pass_both(1, g, (1,), both_halves)
        settle(1, 3 - z, (1,))

    def sent(r, b):
        for kc in range(4):
            @pl.when(kc <= r)
            def _():
                @pl.when((r <= z) & (z < 3))
                def _():
                    t_up(r, kc, b).wait_send()

                @pl.when((r >= z) & (z > 0))
                def _():
                    t_dn(r, kc, b).wait_send()

                t_xn(r, kc, b).wait_send()
                t_sib(r, kc, b).wait_send()
                t_fwd(r, kc, b).wait_send()
        pin(z, r, b).wait_send()
        for m in (0, 1):
            px(0, c, r, b, m).wait_send()
            px(1, c, r, b, m).wait_send()
            px(2, xn, r, b, m).wait_send()

        @pl.when(is_mid)
        def _():
            pout(z, r, b).wait_send()
            for m in (0, 1):
                rshare(0, c, r, b, m).wait_send()
                rshare(1, xn, r, b, m).wait_send()
                pfwd(e, r, b, m).wait_send()

        @pl.when(is_end)
        def _():
            for m in (0, 1):
                rup(r, b, m).wait_send()

    @pl.loop(0, 4)
    def _(r):
        for b in range(nb):
            sent(r, b)

    for h in (0, 1):
        for m in (0, 1):
            rs(z, h, m).wait_send()
            rs(z + 1 - 2 * (z // 2), h, m).wait_send()

            @pl.when(is_mid)
            def _():
                rs(e, h, m).wait_send()
                rs(f, h, m).wait_send()
                for k in (0, 1):
                    dm(k, 0, h, m).wait_send()
                    dm(k, 1, h, m).wait_send()

            @pl.when(is_end)
            def _():
                yf(0, h, m).wait_send()
                yf(1, h, m).wait_send()


def single(nb, fac, piv, c_hbm, out, tbuf, cbuf, chi, clo, acc, colbuf, rowt, obuf,
           csem, tss, trs, pzs, pzr, phs, phr, pxs, pxr, osem):
    g, z, c = lax.axis_index("grp"), lax.axis_index("row"), lax.axis_index("col")
    sib = c + 1 - 2 * (c % 2)
    xn = (c + 2) % 4
    d_up, d_dn = (g, z + 1, c), (g, z - 1, c)
    d_xn, d_sib = (g, z, xn), (g, z, sib)
    piece = fac.shape[1]

    def order(zz, j):
        if j == 0:
            return zz
        if j == 1:
            return zz - 1 + 2 * ((3 - zz) // 3)
        if j == 2:
            return zz + 1 + (3 - zz) // 3 - 3 * (zz // 3)
        return 3 - 3 * (zz // 2)

    cload = pltpu.make_async_copy(c_hbm, cbuf, csem)
    cload.start()

    bar = pltpu.get_barrier_semaphore()

    def hello(dev):
        pl.semaphore_signal(bar, inc=1, device_id=dev, device_id_type=MESH)

    hello(d_xn)
    hello(d_sib)

    @pl.when(z < 3)
    def _():
        hello(d_up)

    @pl.when(z > 0)
    def _():
        hello(d_dn)

    for kc in range(4):
        @pl.when(kc <= z)
        def _():
            start = W * z + piece * c
            rows = start + lax.broadcasted_iota(jnp.int32, (piece, W), 0)
            cols = W * kc + lax.broadcasted_iota(jnp.int32, (piece, W), 1)
            for b in range(nb):
                diag = jnp.where(cols == rows, jnp.broadcast_to(piv[b:b + 1, :], (piece, W)), 0.0)
                tbuf[kc, b, pl.ds(pl.multiple_of(start, piece), piece), :] = jnp.where(
                    cols < rows, fac[b, :, W * kc:W * (kc + 1)], diag)

    pl.semaphore_wait(bar, 2 + (z + 3) // 4 + 1 - z // 3)

    def remote(ref, ss, rs, dev):
        return pltpu.make_async_remote_copy(
            src_ref=ref, dst_ref=ref, send_sem=ss, recv_sem=rs, device_id=dev, device_id_type=MESH)

    def tcopy(route, arrive, r, kc, col, dev):
        ref = tbuf.at[kc, :, pl.ds(pl.multiple_of(W * r + piece * col, piece), piece), :]
        return remote(ref, tss.at[route, r, kc], trs.at[arrive, r, kc], dev)

    def t_up(r, kc):
        return tcopy(0, 0, r, kc, c, d_up)

    def t_dn(r, kc):
        return tcopy(1, 0, r, kc, c, d_dn)

    def t_xn(r, kc):
        return tcopy(2, 1, r, kc, c, d_xn)

    def t_sib(r, kc):
        return tcopy(3, 2, r, kc, c, d_sib)

    def t_fwd(r, kc):
        return tcopy(4, 3, r, kc, xn, d_sib)

    def t_first(j):
        r = order(z, j)

        @pl.loop(0, r + 1)
        def _(kc):
            if j > 0:
                t_up(r, kc).wait_recv()

            @pl.when((r <= z) & (z < 3))
            def _():
                t_up(r, kc).start()

            @pl.when((r >= z) & (z > 0))
            def _():
                t_dn(r, kc).start()

            t_xn(r, kc).start()
            t_sib(r, kc).start()

    def t_second(j):
        r = order(z, j)

        @pl.loop(0, r + 1)
        def _(kc):
            t_xn(r, kc).wait_recv()
            t_fwd(r, kc).start()

    def pz(s, rg, up):
        return remote(colbuf.at[s, rg], pzs.at[0 if up else 1, s, rg], pzr.at[s, rg], d_up if up else d_dn)

    def px(route, col, rg):
        return remote(rowt.at[col, rg], pxs.at[route, rg], pxr.at[route, rg], d_xn if route == 0 else d_sib)

    def project(j):
        r = order(z, j)

        @pl.loop(0, r + 1)
        def _(kc):
            t_sib(r, kc).wait_recv()
            t_fwd(r, kc).wait_recv()

        rows = pl.ds(pl.multiple_of(W * r, W), W)
        for b in range(nb):
            acc[...] = jnp.zeros_like(acc)

            @pl.loop(0, r + 1)
            def _(kc):
                t = tbuf[kc, b, rows, :]
                th = t.astype(bf16)
                tl = (t - th.astype(f32)).astype(bf16)
                ks = pl.ds(pl.multiple_of(W * kc, W), W)
                ch = chi[b, ks, :]
                acc[...] += (jnp.dot(th, ch, preferred_element_type=f32)
                             + jnp.dot(th, clo[b, ks, :], preferred_element_type=f32)
                             + jnp.dot(tl, ch, preferred_element_type=f32))

            full = acc[...]
            colbuf[z, r, W * b:W * (b + 1), :] = full.astype(bf16)
            rowt[c, r, :, W * b:W * (b + 1)] = full.T.astype(bf16)

        @pl.when(z < 3)
        def _():
            pz(z, r, True).start()

        @pl.when(z > 0)
        def _():
            pz(z, r, False).start()

        px(0, c, r).start()
        px(1, c, r).start()

    t_first(0)
    cload.wait()
    for b in range(nb):
        cc = cbuf[b]
        hi = cc.astype(bf16)
        chi[b] = hi
        clo[b] = (cc - hi.astype(f32)).astype(bf16)
    t_first(1)
    t_first(2)
    t_second(0)
    project(0)
    t_first(3)
    t_second(1)
    project(1)
    t_second(2)
    project(2)
    t_second(3)
    project(3)

    H = W // 2

    def block(cp, s, lo, n):
        total = jnp.dot(rowt[cp, 0], colbuf[s, 0, :, lo:lo + n], preferred_element_type=f32)
        for rg in range(1, 4):
            total += jnp.dot(rowt[cp, rg], colbuf[s, rg, :, lo:lo + n], preferred_element_type=f32)
        return total

    def emit(s, h):
        cols = pl.ds(pl.multiple_of(W * s + H * h, H), H)
        return pltpu.make_async_copy(obuf.at[:, cols], out.at[:, cols], osem.at[s, h])

    def gram(s, halves):
        lo, n = H * halves[0], H * len(halves)
        cols = pl.ds(pl.multiple_of(W * s + lo, H), n)
        @pl.loop(0, 4)
        def _(i):
            obuf[pl.ds(pl.multiple_of(W * i, W), W), cols] = block(i, s, lo, n)

    def finish(s):
        for h in (0, 1):
            emit(s, h).start()

    def ph(s, rg, h, up):
        return remote(colbuf.at[s, rg, :, H * h:H * (h + 1)], phs.at[rg, h], phr.at[rg, h], d_up if up else d_dn)

    def near(i):
        lo, hi = z - 1, z + 1

        @pl.when(lo >= 0)
        def _():
            rg = order(lo, i)
            pz(lo, rg, True).wait_recv()

            @pl.when(z < 3)
            def _():
                pz(lo, rg, True).start()

        @pl.when(hi <= 3)
        def _():
            rg = order(hi, i)
            pz(hi, rg, False).wait_recv()

            @pl.when(z > 0)
            def _():
                pz(hi, rg, False).start()

    def second(s, up):
        for i in range(4):
            pz(s, order(s, i), up).wait_recv()

        @pl.when((z == 1) | (z == 2))
        def _():
            for h in (0, 1):
                for rg in range(4):
                    ph(s, rg, h, up).start()

        gram(s, (0, 1))

    def third(s, up):
        for h in (0, 1):
            for rg in range(4):
                ph(s, rg, h, up).wait_recv()
            gram(s, (h,))

    def each(d, fn):
        @pl.when(z - d >= 0)
        def _():
            fn(z - d, True)

        @pl.when(z + d <= 3)
        def _():
            fn(z + d, False)

    for i in range(4):
        near(i)
        r = order(z, i)
        px(0, c, r).wait_recv()
        px(2, xn, r).start()
    for i in range(4):
        px(1, c, i).wait_recv()
        px(2, c, i).wait_recv()
    gram(z, (0, 1))
    each(1, lambda s, up: gram(s, (0, 1)))
    each(2, second)
    finish(z)
    each(1, lambda s, up: finish(s))
    each(3, third)
    each(2, lambda s, up: finish(s))
    each(3, lambda s, up: finish(s))

    for r in range(4):
        for kc in range(r + 1):
            @pl.when((r <= z) & (z < 3))
            def _():
                t_up(r, kc).wait_send()

            @pl.when((r >= z) & (z > 0))
            def _():
                t_dn(r, kc).wait_send()

            t_xn(r, kc).wait_send()
            t_sib(r, kc).wait_send()
            t_fwd(r, kc).wait_send()
        for s in range(4):
            @pl.when((s <= z) & (z < 3) & (z - s < 2))
            def _():
                pz(s, r, True).wait_send()

            @pl.when((s >= z) & (z > 0) & (s - z < 2))
            def _():
                pz(s, r, False).wait_send()

        px(0, c, r).wait_send()
        px(1, c, r).wait_send()
        px(2, xn, r).wait_send()
        for h in (0, 1):
            @pl.when((z == 1) | (z == 2))
            def _():
                ph(3, r, h, False).wait_send()

            emit(r, h).wait()


LIMIT = 50


def body(groups, factor, pivots, constraints):
    nb, piece, order_m = factor.shape
    strip = constraints.shape[2]
    assert strip == W and order_m == 4 * W and piece * 4 == W
    dma = pltpu.SemaphoreType.DMA
    wide = [
        pltpu.VMEM((4, nb, 4 * W, W), f32),
        pltpu.VMEM((nb, 4 * W, W), f32),
        pltpu.VMEM((nb, 4 * W, W), bf16),
        pltpu.VMEM((nb, 4 * W, W), bf16),
        pltpu.VMEM((W, W), f32),
    ]
    vmem, anywhere = pl.BlockSpec(memory_space=pltpu.VMEM), pl.BlockSpec(memory_space=pl.ANY)
    if groups == 2:
        kernel, rows_out, limit = paired, 2 * W, LIMIT
        in_specs, out_specs = [anywhere] * 3, vmem
        scratch = [pltpu.VMEM((nb, piece, 4 * W), f32), pltpu.VMEM((nb, piece), f32)] + wide + [
            pltpu.VMEM((4, 4, nb, W, W), bf16),
            pltpu.VMEM((4, 4, nb, W, W), bf16),
            pltpu.VMEM((4, 4, nb, W, W), bf16),
            pltpu.VMEM((4, 2, 2, W, H), bf16),
            pltpu.VMEM((4, 2, 2, W, H), bf16),
            pltpu.VMEM((2, 2, 2, 2, W, H), bf16),
            pltpu.VMEM((2, 2, 2, 2, W, H), bf16),
            pltpu.VMEM((2, 2, 2, W, H), bf16),
            dma((3,)),
            dma((5, 4, 4, nb)),
            dma((4, 4, 4, nb)),
            dma((4, nb)),
            dma((4, 4, nb)),
            dma((4, nb)),
            dma((4, nb)),
            dma((4, nb, 2)),
            dma((4, nb, 2)),
            dma((3, 4, nb, 2)),
            dma((3, 4, nb, 2)),
            dma((4, nb, 2)),
            dma((4, nb, 2)),
            dma((2, 4, nb, 2)),
            dma((2, 4, nb, 2)),
            dma((4, 2, 2)),
            dma((4, 2, 2)),
            dma((2, 2, 2, 2)),
            dma((2, 2, 2, 2)),
            dma((2, 2, 2)),
            dma((2, 2, 2)),
        ]
    else:
        kernel, rows_out, limit = single, 4 * W, 52
        pivots = jnp.tile(pivots, (1, 4))
        in_specs, out_specs = [vmem, vmem, anywhere], anywhere
        scratch = wide + [
            pltpu.VMEM((4, 4, nb * W, W), bf16),
            pltpu.VMEM((4, 4, W, nb * W), bf16),
            pltpu.VMEM((rows_out, 4 * W), f32),
            dma,
            dma((5, 4, 4)),
            dma((4, 4, 4)),
            dma((2, 4, 4)),
            dma((4, 4)),
            dma((4, 2)),
            dma((4, 2)),
            dma((3, 4)),
            dma((3, 4)),
            dma((4, 2)),
        ]
    result = pl.pallas_call(
        functools.partial(kernel, nb),
        out_shape=jax.ShapeDtypeStruct((rows_out, 4 * W), f32),
        in_specs=in_specs,
        out_specs=out_specs,
        scratch_shapes=scratch,
        compiler_params=pltpu.CompilerParams(
            collective_id=0, has_side_effects=True, vmem_limit_bytes=limit << 20),
    )(factor, pivots, constraints)
    if groups != 2:
        result = lax.psum_scatter(result, "grp", scatter_dimension=0, tiled=True)
    return result[None]


def solution(mesh):
    in_specs = (
        P("grp", ("row", "col"), None),
        P("grp", ("row", "col")),
        P("grp", None, ("col", "row")),
    )
    return jax.shard_map(
        functools.partial(body, mesh.shape["grp"]), mesh=mesh, in_specs=in_specs,
        out_specs=P("row", "grp", "col"), check_vma=False)
```

```python
import functools
import jax
import jax.numpy as jnp
from jax import lax
from jax.experimental import pallas as pl
from jax.experimental.pallas import tpu as pltpu
from jax.sharding import PartitionSpec as P

MESH = pl.DeviceIdType.MESH
f32 = jnp.float32
bf16 = jnp.bfloat16
W = 256


H = W // 2
TOP = 2.0 ** 30
LEAST = 1e-25


def encode(t, scale):
    a = t * (scale * TOP)
    return (a * jnp.abs(a) * (a * a)).astype(bf16)


def decode(w, scale):
    a = w.astype(f32)
    root = jnp.sqrt(jnp.sqrt(jnp.abs(a))) * (1.0 / (scale * TOP))
    return jnp.where(a < 0, -root, root)


def order(zz, j):
    if j == 0:
        return zz
    if j == 1:
        return zz - 1 + 2 * ((3 - zz) // 3)
    if j == 2:
        return zz + 1 + (3 - zz) // 3 - 3 * (zz // 3)
    return 3 - 3 * (zz // 2)


def paired(nb, fac, piv, c_hbm, out, tbuf, cbuf, chi, clo, acc, raw, colbuf, rowt, rowe, sbuf, rbuf,
           dsb, drb, yrb, csem, tss, trs, pis, pir, pos, por, pfs, pfr, pxs, pxr, res, rer, rcs, rcr, rss, rsr,
           dms, dmr, yfs, yfr):
    g, z, c = lax.axis_index("grp"), lax.axis_index("row"), lax.axis_index("col")
    sib = c + 1 - 2 * (c % 2)
    xn = (c + 2) % 4
    xs = (sib + 2) % 4
    xp = c // 2
    d_up, d_dn = (g, z + 1, c), (g, z - 1, c)
    d_xn, d_sib = (g, z, xn), (g, z, sib)
    d_y = (1 - g, z, c)
    e = 3 * (z // 2)
    f = 3 - e
    o = 3 - z
    d_in = (g, z + 1 - 2 * (z // 2), c)
    d_end = (g, e, c)
    is_mid = (z == 1) | (z == 2)
    is_end = (z == 0) | (z == 3)
    piece = fac.shape[1]

    cload = pltpu.make_async_copy(c_hbm, cbuf, csem)
    cload.start()

    bar = pltpu.get_barrier_semaphore()

    def hello(dev):
        pl.semaphore_signal(bar, inc=1, device_id=dev, device_id_type=MESH)

    hello(d_xn)
    hello(d_sib)
    hello(d_y)

    @pl.when(z < 3)
    def _():
        hello(d_up)

    @pl.when(z > 0)
    def _():
        hello(d_dn)

    for kc in range(4):
        @pl.when(kc <= z)
        def _():
            start = W * z + piece * c
            rows = start + lax.broadcasted_iota(jnp.int32, (piece, W), 0)
            cols = W * kc + lax.broadcasted_iota(jnp.int32, (piece, W), 1)
            for b in range(nb):
                own = jnp.concatenate([piv[b:b + 1, :]] * (W // piece), axis=1)
                diag = jnp.where(cols == rows, jnp.broadcast_to(own, (piece, W)), 0.0)
                tbuf[kc, b, pl.ds(pl.multiple_of(start, piece), piece), :] = jnp.where(
                    cols < rows, fac[b, :, W * kc:W * (kc + 1)], diag)

    pl.semaphore_wait(bar, 3 + (z + 3) // 4 + 1 - z // 3)

    def remote(src, dst, ss, rs, dev):
        return pltpu.make_async_remote_copy(
            src_ref=src, dst_ref=dst, send_sem=ss, recv_sem=rs, device_id=dev, device_id_type=MESH)

    def tcopy(route, arrive, r, kc, b, col, dev):
        ref = tbuf.at[kc, b, pl.ds(pl.multiple_of(W * r + piece * col, piece), piece), :]
        return remote(ref, ref, tss.at[route, r, kc, b], trs.at[arrive, r, kc, b], dev)

    def t_up(r, kc, b):
        return tcopy(0, 0, r, kc, b, c, d_up)

    def t_dn(r, kc, b):
        return tcopy(1, 0, r, kc, b, c, d_dn)

    def t_xn(r, kc, b):
        return tcopy(2, 1, r, kc, b, c, d_xn)

    def t_sib(r, kc, b):
        return tcopy(3, 2, r, kc, b, c, d_sib)

    def t_fwd(r, kc, b):
        return tcopy(4, 3, r, kc, b, xn, d_sib)

    def t_first(j, b):
        r = order(z, j)

        @pl.loop(0, r + 1)
        def _(kc):
            if j > 0:
                t_up(r, kc, b).wait_recv()

            @pl.when((r <= z) & (z < 3))
            def _():
                t_up(r, kc, b).start()

            @pl.when((r >= z) & (z > 0))
            def _():
                t_dn(r, kc, b).start()

            t_xn(r, kc, b).start()
            t_sib(r, kc, b).start()

    def t_second(j, b):
        r = order(z, j)

        @pl.loop(0, r + 1)
        def _(kc):
            t_xn(r, kc, b).wait_recv()
            t_fwd(r, kc, b).start()

    def pin(s, r, b):
        ref = colbuf.at[s, r, b]
        return remote(ref, ref, pis.at[r, b], pir.at[s, r, b], d_in)

    def pout(s, r, b):
        ref = colbuf.at[s, r, b]
        return remote(ref, ref, pos.at[r, b], por.at[r, b], d_end)

    def pfwd(s, r, b, h):
        ref = colbuf.at[s, r, b, :, H * h:H * (h + 1)]
        return remote(ref, ref, pfs.at[r, b, h], pfr.at[r, b, h], d_in)

    def px(route, col, r, b, m):
        ref = rowt.at[col, r, b, H * m:H * (m + 1), :]
        return remote(ref, ref, pxs.at[route, r, b, m], pxr.at[route, r, b, m], d_xn if route == 0 else d_sib)

    def rup(r, b, m):
        part = (xn, r, b, slice(H * m, H * (m + 1)), slice(None))
        return remote(rowt.at[part], rowe.at[part], res.at[r, b, m], rer.at[r, b, m], d_in)

    def rshare(route, col, r, b, m):
        ref = rowe.at[col, r, b, H * m:H * (m + 1), :]
        return remote(ref, ref, rcs.at[route, r, b, m], rcr.at[route, r, b, m], d_sib)

    def rs(s, h, m):
        return remote(sbuf.at[s, h, m], rbuf.at[s, h, m], rss.at[s, h, m], rsr.at[s, h, m], d_y)

    def dm(k, p, h, m):
        return remote(dsb.at[k, p, h, m], drb.at[k, p, h, m], dms.at[k, p, h, m], dmr.at[k, p, h, m], d_end)

    def yf(k, h, m):
        return remote(drb.at[k, 1 - g, h, m], yrb.at[k, h, m], yfs.at[k, h, m], yfr.at[k, h, m], d_y)

    def project(j, b):
        r = order(z, j)
        rows = pl.ds(pl.multiple_of(W * r, W), W)

        @pl.loop(0, r + 1)
        def _(kc):
            t_sib(r, kc, b).wait_recv()
            t_fwd(r, kc, b).wait_recv()

        acc[...] = jnp.zeros_like(acc)

        @pl.loop(0, r + 1)
        def _(kc):
            t = tbuf[kc, b, rows, :]
            th = t.astype(bf16)
            tl = (t - th.astype(f32)).astype(bf16)
            ks = pl.ds(pl.multiple_of(W * kc, W), W)
            ch = chi[b, ks, :]
            acc[...] += (jnp.dot(th, ch, preferred_element_type=f32)
                         + jnp.dot(th, clo[b, ks, :], preferred_element_type=f32)
                         + jnp.dot(tl, ch, preferred_element_type=f32))

        full = acc[...]
        colbuf[z, r, b] = full.astype(bf16)
        pin(z, r, b).start()
        rowt[c, r, b] = full.T.astype(bf16)

    def split(b):
        cc = cbuf[b]
        hi = cc.astype(bf16)
        chi[b] = hi
        clo[b] = (cc - hi.astype(f32)).astype(bf16)

    def near(m):
        def fn(r, b):
            px(0, c, r, b, m).wait_recv()
            px(2, xn, r, b, m).start()

            @pl.when(is_end)
            def _():
                rup(r, b, m).start()
        return fn

    def strip(r, b):
        pin(e, r, b).wait_recv()
        pfwd(e, r, b, 0).start()
        rowe[c, r, b] = colbuf[e, r, b].astype(f32).T.astype(bf16)
        rshare(0, c, r, b, 0).start()
        rshare(0, c, r, b, 1).start()

    def both(fn, zz, i):
        r = order(zz, i)
        for b in range(nb):
            fn(r, b)

    def first(j):
        for b in range(nb):
            t_first(j, b)

    def get(j):
        for b in range(nb):
            t_second(j, b)
            project(j, b)

    def across(m):
        def fn(r, b):
            px(0, c, r, b, m).start()
            px(1, c, r, b, m).start()
        return fn

    def outward(r, b):
        @pl.when(is_mid)
        def _():
            pout(z, r, b).start()

    first(0)
    cload.wait()
    t_first(1, 0)
    split(0)
    t_first(1, 1)
    split(1)

    @pl.when(is_end)
    def _():
        get(0)

    first(2)

    @pl.when(is_mid)
    def _():
        get(0)

    get(1)
    first(3)

    @pl.when(is_mid)
    def _():
        both(strip, e, 0)

    get(2)
    for i in range(3):
        both(across(0), z, i)

    @pl.when(is_mid)
    def _():
        both(strip, e, 1)

    get(3)
    both(across(0), z, 3)
    for i in range(4):
        both(outward, z, i)
        both(across(1), z, i)

    def block(lhs, cp, ro, rn, s, lo, n):
        total = jnp.dot(lhs[cp, 0, 0, ro:ro + rn, :], colbuf[s, 0, 0, :, lo:lo + n], preferred_element_type=f32)
        for k in range(1, 4 * nb):
            total += jnp.dot(lhs[cp, k // nb, k % nb, ro:ro + rn, :], colbuf[s, k // nb, k % nb, :, lo:lo + n],
                             preferred_element_type=f32)
        return total

    both_halves = (0, 1)

    def coded(lhs, p, s, halves, ms, ref, at):
        lo, n, ro, rn = H * halves[0], H * len(halves), H * ms[0], H * len(ms)

        def tile(i, top):
            t = block(lhs, 2 * p + i, ro, rn, s, lo, n)
            raw[i, 0:rn, 0:n] = t
            return jnp.maximum(top, jnp.max(jnp.abs(t), axis=0, keepdims=True))

        top = lax.fori_loop(0, 2, tile, jnp.full((1, n), LEAST, f32))
        scale = jnp.broadcast_to(1.0 / top, (16, n)).astype(bf16)
        factor = scale[0:1, :].astype(f32)

        @pl.loop(0, 2)
        def _(i):
            t = encode(raw[i, 0:rn, 0:n], factor)
            for q, h in enumerate(halves):
                for u, m in enumerate(ms):
                    ref[(*at, h, m, pl.ds(pl.multiple_of(H * i, H), H), slice(None))] = (
                        t[H * u:H * (u + 1), H * q:H * (q + 1)])

        for q, h in enumerate(halves):
            for m in ms:
                ref[(*at, h, m, slice(W, W + 16), slice(None))] = scale[:, H * q:H * (q + 1)]

    def read(ref, at, part):
        return decode(ref[(*at, part, slice(None))], ref[(*at, slice(W, W + 16), slice(None))].astype(f32)[0:1, :])

    def send(s, halves, ms):
        coded(rowt, 1 - g, s, halves, ms, sbuf, (s,))
        for h in halves:
            for m in ms:
                rs(s, h, m).start()

    def lend(k, s, p, halves, ms):
        coded(rowe, p, s, halves, ms, dsb, (k, p))
        for h in halves:
            for m in ms:
                dm(k, p, h, m).start()

    def keep(s, ms):
        cols, ro, rn = pl.ds(pl.multiple_of(W * s, W), W), H * ms[0], H * len(ms)

        @pl.loop(0, 2)
        def _(i):
            out[pl.ds(pl.multiple_of(W * i + ro, H), rn), cols] = block(rowt, 2 * g + i, ro, rn, s, 0, W)

    def work(s, p, ms):
        @pl.when(p == g)
        def _():
            keep(s, ms)

        @pl.when(p != g)
        def _():
            send(s, both_halves, ms)

    def parts(s):
        for h in (0, 1):
            cols = pl.ds(pl.multiple_of(W * s + H * h, H), H)
            for m in (0, 1):
                for i in (0, 1):
                    yield h, m, i, slice(W * i + H * m, W * i + H * (m + 1)), cols, slice(H * i, H * (i + 1))

    def finish(s):
        for h, m, i, rows, cols, part in parts(s):
            if i == 0:
                rs(s, h, m).wait_recv()
            out[rows, cols] = out[rows, cols] + read(rbuf, (s, h, m), part)

    def settle(k, s, hs):
        for h, m, i, rows, cols, part in parts(s):
            if h in hs:
                if i == 0:
                    yf(k, h, m).wait_recv()
                out[rows, cols] = read(drb, (k, g, h, m), part) + read(yrb, (k, h, m), part)

    def pass_on(k, p, h, m):
        dm(k, p, h, m).wait_recv()

        @pl.when(p != g)
        def _():
            yf(k, h, m).start()

    def every(fn):
        for r in range(4):
            for b in range(nb):
                fn(r, b)

    def sib_rows():
        for m in (0, 1):
            every(lambda r, b: px(1, sib, r, b, m).wait_recv())

    def far_rows(m):
        every(lambda r, b: px(2, xs, r, b, m).wait_recv())

    def lent_rows(route, col, ms):
        for m in ms:
            every(lambda r, b: rshare(route, col, r, b, m).wait_recv())

    @pl.when(is_mid)
    def _():
        def turn(m):
            def fn(r, b):
                rup(r, b, m).wait_recv()
                rshare(1, xn, r, b, m).start()
            return fn

        sib_rows()
        work(z, xp, both_halves)
        both(near(0), z, 0)
        both(near(0), z, 1)
        both(strip, e, 2)
        both(near(0), z, 2)
        both(strip, e, 3)
        for i in range(4):
            both(lambda r, b: pfwd(e, r, b, 1).start(), e, i)
        both(near(0), z, 3)
        work(e, xp, both_halves)
        far_rows(0)
        work(z, 1 - xp, (0,))
        work(e, 1 - xp, (0,))
        for i in range(4):
            both(lambda r, b: pin(o, r, b).wait_recv(), o, i)
        lent_rows(0, sib, both_halves)
        lend(0, o, xp, both_halves, both_halves)
        both(near(1), z, 0)
        both(near(1), z, 1)
        work(o, 1 - xp, (0,))
        for i in range(4):
            if i >= 2:
                both(near(1), z, i)
            both(turn(0), e, i)
        far_rows(1)
        for s in (z, e, o):
            work(s, 1 - xp, (1,))
        lent_rows(1, xs, (0,))
        lend(0, o, 1 - xp, both_halves, (0,))
        for i in range(4):
            both(lambda r, b: pfwd(f, r, b, 0).wait_recv(), f, i)
        lend(1, f, xp, (0,), both_halves)
        lend(1, f, 1 - xp, (0,), (0,))
        work(o, xp, both_halves)
        for i in range(4):
            both(turn(1), e, i)
        lent_rows(1, xs, (1,))
        lend(0, o, 1 - xp, both_halves, (1,))
        lend(1, f, 1 - xp, (0,), (1,))
        finish(z)
        finish(e)
        for i in range(4):
            both(lambda r, b: pfwd(f, r, b, 1).wait_recv(), f, i)
        lend(1, f, 1 - g, (1,), both_halves)
        lend(1, f, g, (1,), both_halves)
        send(f, both_halves, both_halves)
        keep(f, both_halves)
        finish(o)
        finish(f)

    @pl.when(is_end)
    def _():
        inner = 1 + z // 3
        both(near(0), z, 0)
        sib_rows()
        work(z, xp, both_halves)
        for i in range(1, 4):
            both(near(0), z, i)
        far_rows(0)
        work(z, 1 - xp, (0,))
        both(near(1), z, 0)
        both(near(1), z, 1)
        for i in range(4):
            both(lambda r, b: pout(inner, r, b).wait_recv(), inner, i)
        work(inner, 1 - xp, (0,))
        both(near(1), z, 2)
        both(near(1), z, 3)
        far_rows(1)
        work(z, 1 - xp, (1,))
        work(inner, 1 - xp, (1,))
        work(inner, xp, both_halves)

        def pass_both(k, p, hs, ms):
            for h in hs:
                for m in ms:
                    pass_on(k, p, h, m)

        pass_both(0, xp, both_halves, both_halves)
        pass_both(0, 1 - xp, both_halves, (0,))
        pass_both(1, xp, (0,), both_halves)
        pass_both(1, 1 - xp, (0,), (0,))
        finish(z)
        finish(inner)
        pass_both(0, 1 - xp, both_halves, (1,))
        pass_both(1, 1 - xp, (0,), (1,))
        settle(0, 3 - inner, both_halves)
        pass_both(1, 1 - g, (1,), both_halves)
        settle(1, 3 - z, (0,))
        pass_both(1, g, (1,), both_halves)
        settle(1, 3 - z, (1,))

    def sent(r, b):
        for kc in range(4):
            @pl.when(kc <= r)
            def _():
                @pl.when((r <= z) & (z < 3))
                def _():
                    t_up(r, kc, b).wait_send()

                @pl.when((r >= z) & (z > 0))
                def _():
                    t_dn(r, kc, b).wait_send()

                t_xn(r, kc, b).wait_send()
                t_sib(r, kc, b).wait_send()
                t_fwd(r, kc, b).wait_send()
        pin(z, r, b).wait_send()
        for m in (0, 1):
            px(0, c, r, b, m).wait_send()
            px(1, c, r, b, m).wait_send()
            px(2, xn, r, b, m).wait_send()

        @pl.when(is_mid)
        def _():
            pout(z, r, b).wait_send()
            for m in (0, 1):
                rshare(0, c, r, b, m).wait_send()
                rshare(1, xn, r, b, m).wait_send()
                pfwd(e, r, b, m).wait_send()

        @pl.when(is_end)
        def _():
            for m in (0, 1):
                rup(r, b, m).wait_send()

    @pl.loop(0, 4)
    def _(r):
        for b in range(nb):
            sent(r, b)

    for h in (0, 1):
        for m in (0, 1):
            rs(z, h, m).wait_send()
            rs(z + 1 - 2 * (z // 2), h, m).wait_send()

            @pl.when(is_mid)
            def _():
                rs(e, h, m).wait_send()
                rs(f, h, m).wait_send()
                for k in (0, 1):
                    dm(k, 0, h, m).wait_send()
                    dm(k, 1, h, m).wait_send()

            @pl.when(is_end)
            def _():
                yf(0, h, m).wait_send()
                yf(1, h, m).wait_send()


def single(nb, fac, piv, c_hbm, out, tbuf, cbuf, chi, clo, acc, colbuf, rowt, obuf,
           csem, tss, trs, pzs, pzr, phs, phr, pxs, pxr, osem):
    g, z, c = lax.axis_index("grp"), lax.axis_index("row"), lax.axis_index("col")
    sib = c + 1 - 2 * (c % 2)
    xn = (c + 2) % 4
    d_up, d_dn = (g, z + 1, c), (g, z - 1, c)
    d_xn, d_sib = (g, z, xn), (g, z, sib)
    piece = fac.shape[1]

    def order(zz, j):
        if j == 0:
            return zz
        if j == 1:
            return zz - 1 + 2 * ((3 - zz) // 3)
        if j == 2:
            return zz + 1 + (3 - zz) // 3 - 3 * (zz // 3)
        return 3 - 3 * (zz // 2)

    cload = pltpu.make_async_copy(c_hbm, cbuf, csem)
    cload.start()

    bar = pltpu.get_barrier_semaphore()

    def hello(dev):
        pl.semaphore_signal(bar, inc=1, device_id=dev, device_id_type=MESH)

    hello(d_xn)
    hello(d_sib)

    @pl.when(z < 3)
    def _():
        hello(d_up)

    @pl.when(z > 0)
    def _():
        hello(d_dn)

    for kc in range(4):
        @pl.when(kc <= z)
        def _():
            start = W * z + piece * c
            rows = start + lax.broadcasted_iota(jnp.int32, (piece, W), 0)
            cols = W * kc + lax.broadcasted_iota(jnp.int32, (piece, W), 1)
            for b in range(nb):
                diag = jnp.where(cols == rows, jnp.broadcast_to(piv[b:b + 1, :], (piece, W)), 0.0)
                tbuf[kc, b, pl.ds(pl.multiple_of(start, piece), piece), :] = jnp.where(
                    cols < rows, fac[b, :, W * kc:W * (kc + 1)], diag)

    pl.semaphore_wait(bar, 2 + (z + 3) // 4 + 1 - z // 3)

    def remote(ref, ss, rs, dev):
        return pltpu.make_async_remote_copy(
            src_ref=ref, dst_ref=ref, send_sem=ss, recv_sem=rs, device_id=dev, device_id_type=MESH)

    def tcopy(route, arrive, r, kc, col, dev):
        ref = tbuf.at[kc, :, pl.ds(pl.multiple_of(W * r + piece * col, piece), piece), :]
        return remote(ref, tss.at[route, r, kc], trs.at[arrive, r, kc], dev)

    def t_up(r, kc):
        return tcopy(0, 0, r, kc, c, d_up)

    def t_dn(r, kc):
        return tcopy(1, 0, r, kc, c, d_dn)

    def t_xn(r, kc):
        return tcopy(2, 1, r, kc, c, d_xn)

    def t_sib(r, kc):
        return tcopy(3, 2, r, kc, c, d_sib)

    def t_fwd(r, kc):
        return tcopy(4, 3, r, kc, xn, d_sib)

    def t_first(j):
        r = order(z, j)

        @pl.loop(0, r + 1)
        def _(kc):
            if j > 0:
                t_up(r, kc).wait_recv()

            @pl.when((r <= z) & (z < 3))
            def _():
                t_up(r, kc).start()

            @pl.when((r >= z) & (z > 0))
            def _():
                t_dn(r, kc).start()

            t_xn(r, kc).start()
            t_sib(r, kc).start()

    def t_second(j):
        r = order(z, j)

        @pl.loop(0, r + 1)
        def _(kc):
            t_xn(r, kc).wait_recv()
            t_fwd(r, kc).start()

    def pz(s, rg, up):
        return remote(colbuf.at[s, rg], pzs.at[0 if up else 1, s, rg], pzr.at[s, rg], d_up if up else d_dn)

    def px(route, col, rg):
        return remote(rowt.at[col, rg], pxs.at[route, rg], pxr.at[route, rg], d_xn if route == 0 else d_sib)

    def project(j):
        r = order(z, j)

        @pl.loop(0, r + 1)
        def _(kc):
            t_sib(r, kc).wait_recv()
            t_fwd(r, kc).wait_recv()

        rows = pl.ds(pl.multiple_of(W * r, W), W)
        for b in range(nb):
            acc[...] = jnp.zeros_like(acc)

            @pl.loop(0, r + 1)
            def _(kc):
                t = tbuf[kc, b, rows, :]
                th = t.astype(bf16)
                tl = (t - th.astype(f32)).astype(bf16)
                ks = pl.ds(pl.multiple_of(W * kc, W), W)
                ch = chi[b, ks, :]
                acc[...] += (jnp.dot(th, ch, preferred_element_type=f32)
                             + jnp.dot(th, clo[b, ks, :], preferred_element_type=f32)
                             + jnp.dot(tl, ch, preferred_element_type=f32))

            full = acc[...]
            colbuf[z, r, W * b:W * (b + 1), :] = full.astype(bf16)
            rowt[c, r, :, W * b:W * (b + 1)] = full.T.astype(bf16)

        @pl.when(z < 3)
        def _():
            pz(z, r, True).start()

        @pl.when(z > 0)
        def _():
            pz(z, r, False).start()

        px(0, c, r).start()
        px(1, c, r).start()

    t_first(0)
    cload.wait()
    for b in range(nb):
        cc = cbuf[b]
        hi = cc.astype(bf16)
        chi[b] = hi
        clo[b] = (cc - hi.astype(f32)).astype(bf16)
    t_first(1)
    t_first(2)
    t_second(0)
    project(0)
    t_first(3)
    t_second(1)
    project(1)
    t_second(2)
    project(2)
    t_second(3)
    project(3)

    H = W // 2

    def block(cp, s, lo, n):
        total = jnp.dot(rowt[cp, 0], colbuf[s, 0, :, lo:lo + n], preferred_element_type=f32)
        for rg in range(1, 4):
            total += jnp.dot(rowt[cp, rg], colbuf[s, rg, :, lo:lo + n], preferred_element_type=f32)
        return total

    def emit(s, h):
        cols = pl.ds(pl.multiple_of(W * s + H * h, H), H)
        return pltpu.make_async_copy(obuf.at[:, cols], out.at[:, cols], osem.at[s, h])

    def gram(s, halves):
        lo, n = H * halves[0], H * len(halves)
        cols = pl.ds(pl.multiple_of(W * s + lo, H), n)
        @pl.loop(0, 4)
        def _(i):
            obuf[pl.ds(pl.multiple_of(W * i, W), W), cols] = block(i, s, lo, n)

    def finish(s):
        for h in (0, 1):
            emit(s, h).start()

    def ph(s, rg, h, up):
        return remote(colbuf.at[s, rg, :, H * h:H * (h + 1)], phs.at[rg, h], phr.at[rg, h], d_up if up else d_dn)

    def near(i):
        lo, hi = z - 1, z + 1

        @pl.when(lo >= 0)
        def _():
            rg = order(lo, i)
            pz(lo, rg, True).wait_recv()

            @pl.when(z < 3)
            def _():
                pz(lo, rg, True).start()

        @pl.when(hi <= 3)
        def _():
            rg = order(hi, i)
            pz(hi, rg, False).wait_recv()

            @pl.when(z > 0)
            def _():
                pz(hi, rg, False).start()

    def second(s, up):
        for i in range(4):
            pz(s, order(s, i), up).wait_recv()

        @pl.when((z == 1) | (z == 2))
        def _():
            for h in (0, 1):
                for rg in range(4):
                    ph(s, rg, h, up).start()

        gram(s, (0, 1))

    def third(s, up):
        for h in (0, 1):
            for rg in range(4):
                ph(s, rg, h, up).wait_recv()
            gram(s, (h,))

    def each(d, fn):
        @pl.when(z - d >= 0)
        def _():
            fn(z - d, True)

        @pl.when(z + d <= 3)
        def _():
            fn(z + d, False)

    for i in range(4):
        near(i)
        r = order(z, i)
        px(0, c, r).wait_recv()
        px(2, xn, r).start()
    for i in range(4):
        px(1, c, i).wait_recv()
        px(2, c, i).wait_recv()
    gram(z, (0, 1))
    each(1, lambda s, up: gram(s, (0, 1)))
    each(2, second)
    finish(z)
    each(1, lambda s, up: finish(s))
    each(3, third)
    each(2, lambda s, up: finish(s))
    each(3, lambda s, up: finish(s))

    for r in range(4):
        for kc in range(r + 1):
            @pl.when((r <= z) & (z < 3))
            def _():
                t_up(r, kc).wait_send()

            @pl.when((r >= z) & (z > 0))
            def _():
                t_dn(r, kc).wait_send()

            t_xn(r, kc).wait_send()
            t_sib(r, kc).wait_send()
            t_fwd(r, kc).wait_send()
        for s in range(4):
            @pl.when((s <= z) & (z < 3) & (z - s < 2))
            def _():
                pz(s, r, True).wait_send()

            @pl.when((s >= z) & (z > 0) & (s - z < 2))
            def _():
                pz(s, r, False).wait_send()

        px(0, c, r).wait_send()
        px(1, c, r).wait_send()
        px(2, xn, r).wait_send()
        for h in (0, 1):
            @pl.when((z == 1) | (z == 2))
            def _():
                ph(3, r, h, False).wait_send()

            emit(r, h).wait()


LIMIT = 204


def body(groups, factor, pivots, constraints):
    nb, piece, order_m = factor.shape
    strip = constraints.shape[2]
    assert strip == W and order_m == 4 * W and piece * 4 == W
    dma = pltpu.SemaphoreType.DMA
    wide = [
        pltpu.VMEM((4, nb, 4 * W, W), f32),
        pltpu.VMEM((nb, 4 * W, W), f32),
        pltpu.VMEM((nb, 4 * W, W), bf16),
        pltpu.VMEM((nb, 4 * W, W), bf16),
        pltpu.VMEM((W, W), f32),
    ]
    vmem, anywhere = pl.BlockSpec(memory_space=pltpu.VMEM), pl.BlockSpec(memory_space=pl.ANY)
    if groups == 2:
        kernel, rows_out, limit = paired, 2 * W, LIMIT
        in_specs, out_specs = [vmem, vmem, anywhere], vmem
        scratch = wide + [
            pltpu.VMEM((2, W, W), f32),
            pltpu.VMEM((4, 4, nb, W, W), bf16),
            pltpu.VMEM((4, 4, nb, W, W), bf16),
            pltpu.VMEM((4, 4, nb, W, W), bf16),
            pltpu.VMEM((4, 2, 2, W + 16, H), bf16),
            pltpu.VMEM((4, 2, 2, W + 16, H), bf16),
            pltpu.VMEM((2, 2, 2, 2, W + 16, H), bf16),
            pltpu.VMEM((2, 2, 2, 2, W + 16, H), bf16),
            pltpu.VMEM((2, 2, 2, W + 16, H), bf16),
            dma,
            dma((5, 4, 4, nb)),
            dma((4, 4, 4, nb)),
            dma((4, nb)),
            dma((4, 4, nb)),
            dma((4, nb)),
            dma((4, nb)),
            dma((4, nb, 2)),
            dma((4, nb, 2)),
            dma((3, 4, nb, 2)),
            dma((3, 4, nb, 2)),
            dma((4, nb, 2)),
            dma((4, nb, 2)),
            dma((2, 4, nb, 2)),
            dma((2, 4, nb, 2)),
            dma((4, 2, 2)),
            dma((4, 2, 2)),
            dma((2, 2, 2, 2)),
            dma((2, 2, 2, 2)),
            dma((2, 2, 2)),
            dma((2, 2, 2)),
        ]
    else:
        kernel, rows_out, limit = single, 4 * W, 208
        pivots = jnp.tile(pivots, (1, 4))
        in_specs, out_specs = [vmem, vmem, anywhere], anywhere
        scratch = wide + [
            pltpu.VMEM((4, 4, nb * W, W), bf16),
            pltpu.VMEM((4, 4, W, nb * W), bf16),
            pltpu.VMEM((rows_out, 4 * W), f32),
            dma,
            dma((5, 4, 4)),
            dma((4, 4, 4)),
            dma((2, 4, 4)),
            dma((4, 4)),
            dma((4, 2)),
            dma((4, 2)),
            dma((3, 4)),
            dma((3, 4)),
            dma((4, 2)),
        ]
    result = pl.pallas_call(
        functools.partial(kernel, nb),
        out_shape=jax.ShapeDtypeStruct((rows_out, 4 * W), f32),
        in_specs=in_specs,
        out_specs=out_specs,
        scratch_shapes=scratch,
        compiler_params=pltpu.CompilerParams(
            collective_id=0, has_side_effects=True, vmem_limit_bytes=limit << 18),
    )(factor, pivots, constraints)
    if groups != 2:
        result = lax.psum_scatter(result, "grp", scatter_dimension=0, tiled=True)
    return result[None]


def solution(mesh):
    in_specs = (
        P("grp", ("row", "col"), None),
        P("grp", ("row", "col")),
        P("grp", None, ("col", "row")),
    )
    return jax.shard_map(
        functools.partial(body, mesh.shape["grp"]), mesh=mesh, in_specs=in_specs,
        out_specs=P("row", "grp", "col"), check_vma=False)
```

```python
import functools
import jax
import jax.numpy as jnp
from jax import lax
from jax.experimental import pallas as pl
from jax.experimental.pallas import tpu as pltpu
from jax.sharding import PartitionSpec as P

MESH = pl.DeviceIdType.MESH
f32 = jnp.float32
bf16 = jnp.bfloat16
W = 256


H = W // 2
TOP = 2.0 ** 30
LEAST = 1e-25


def encode(t, scale):
    a = t * (scale * TOP)
    return (a * jnp.abs(a) * (a * a)).astype(bf16)


def decode(w, scale):
    a = w.astype(f32)
    root = jnp.sqrt(jnp.sqrt(jnp.abs(a))) * (1.0 / (scale * TOP))
    return jnp.where(a < 0, -root, root)


def order(zz, j):
    if j == 0:
        return zz
    if j == 1:
        return zz - 1 + 2 * ((3 - zz) // 3)
    if j == 2:
        return zz + 1 + (3 - zz) // 3 - 3 * (zz // 3)
    return 3 - 3 * (zz // 2)


def paired(nb, fac, piv, c_hbm, out, tbuf, cbuf, chi, clo, acc, raw, colbuf, rowt, rowe, sbuf, rbuf,
           dsb, drb, yrb, csem, tss, trs, pis, pir, pos, por, pfs, pfr, pxs, pxr, res, rer, rcs, rcr, rss, rsr,
           dms, dmr, yfs, yfr):
    g, z, c = lax.axis_index("grp"), lax.axis_index("row"), lax.axis_index("col")
    sib = c + 1 - 2 * (c % 2)
    xn = (c + 2) % 4
    xs = (sib + 2) % 4
    xp = c // 2
    d_up, d_dn = (g, z + 1, c), (g, z - 1, c)
    d_xn, d_sib = (g, z, xn), (g, z, sib)
    d_y = (1 - g, z, c)
    e = 3 * (z // 2)
    f = 3 - e
    o = 3 - z
    d_in = (g, z + 1 - 2 * (z // 2), c)
    d_end = (g, e, c)
    is_mid = (z == 1) | (z == 2)
    is_end = (z == 0) | (z == 3)
    piece = fac.shape[1]

    cload = pltpu.make_async_copy(c_hbm, cbuf, csem)
    cload.start()

    bar = pltpu.get_barrier_semaphore()

    def hello(dev):
        pl.semaphore_signal(bar, inc=1, device_id=dev, device_id_type=MESH)

    hello(d_xn)
    hello(d_sib)
    hello(d_y)

    @pl.when(z < 3)
    def _():
        hello(d_up)

    @pl.when(z > 0)
    def _():
        hello(d_dn)

    for kc in range(4):
        @pl.when(kc <= z)
        def _():
            start = W * z + piece * c
            rows = start + lax.broadcasted_iota(jnp.int32, (piece, W), 0)
            cols = W * kc + lax.broadcasted_iota(jnp.int32, (piece, W), 1)
            for b in range(nb):
                own = jnp.concatenate([piv[b:b + 1, :]] * (W // piece), axis=1)
                diag = jnp.where(cols == rows, jnp.broadcast_to(own, (piece, W)), 0.0)
                tbuf[kc, b, pl.ds(pl.multiple_of(start, piece), piece), :] = jnp.where(
                    cols < rows, fac[b, :, W * kc:W * (kc + 1)], diag)

    pl.semaphore_wait(bar, 3 + (z + 3) // 4 + 1 - z // 3)

    def remote(src, dst, ss, rs, dev):
        return pltpu.make_async_remote_copy(
            src_ref=src, dst_ref=dst, send_sem=ss, recv_sem=rs, device_id=dev, device_id_type=MESH)

    def tcopy(route, arrive, r, kc, b, col, dev):
        ref = tbuf.at[kc, b, pl.ds(pl.multiple_of(W * r + piece * col, piece), piece), :]
        return remote(ref, ref, tss.at[route, r, kc, b], trs.at[arrive, r, kc, b], dev)

    def t_up(r, kc, b):
        return tcopy(0, 0, r, kc, b, c, d_up)

    def t_dn(r, kc, b):
        return tcopy(1, 0, r, kc, b, c, d_dn)

    def t_xn(r, kc, b):
        return tcopy(2, 1, r, kc, b, c, d_xn)

    def t_sib(r, kc, b):
        return tcopy(3, 2, r, kc, b, c, d_sib)

    def t_fwd(r, kc, b):
        return tcopy(4, 3, r, kc, b, xn, d_sib)

    def t_first(j, b):
        r = order(z, j)

        @pl.loop(0, r + 1)
        def _(kc):
            if j > 0:
                t_up(r, kc, b).wait_recv()

            @pl.when((r <= z) & (z < 3))
            def _():
                t_up(r, kc, b).start()

            @pl.when((r >= z) & (z > 0))
            def _():
                t_dn(r, kc, b).start()

            t_xn(r, kc, b).start()
            t_sib(r, kc, b).start()

    def t_second(j, b):
        r = order(z, j)

        @pl.loop(0, r + 1)
        def _(kc):
            t_xn(r, kc, b).wait_recv()
            t_fwd(r, kc, b).start()

    def pin(s, r, b):
        ref = colbuf.at[s, r, W * b:W * (b + 1), :]
        return remote(ref, ref, pis.at[r, b], pir.at[s, r, b], d_in)

    def pout(s, r, b):
        ref = colbuf.at[s, r, W * b:W * (b + 1), :]
        return remote(ref, ref, pos.at[r, b], por.at[r, b], d_end)

    def pfwd(s, r, b, h):
        ref = colbuf.at[s, r, W * b:W * (b + 1), H * h:H * (h + 1)]
        return remote(ref, ref, pfs.at[r, b, h], pfr.at[r, b, h], d_in)

    def px(route, col, r, b, m):
        ref = rowt.at[col, r, H * m:H * (m + 1), W * b:W * (b + 1)]
        return remote(ref, ref, pxs.at[route, r, b, m], pxr.at[route, r, b, m], d_xn if route == 0 else d_sib)

    def rup(r, b, m):
        part = (xn, r, slice(H * m, H * (m + 1)), slice(W * b, W * (b + 1)))
        return remote(rowt.at[part], rowe.at[part], res.at[r, b, m], rer.at[r, b, m], d_in)

    def rshare(route, col, r, b, m):
        ref = rowe.at[col, r, H * m:H * (m + 1), W * b:W * (b + 1)]
        return remote(ref, ref, rcs.at[route, r, b, m], rcr.at[route, r, b, m], d_sib)

    def rs(s, h, m):
        return remote(sbuf.at[s, h, m], rbuf.at[s, h, m], rss.at[s, h, m], rsr.at[s, h, m], d_y)

    def dm(k, p, h, m):
        return remote(dsb.at[k, p, h, m], drb.at[k, p, h, m], dms.at[k, p, h, m], dmr.at[k, p, h, m], d_end)

    def yf(k, h, m):
        return remote(drb.at[k, 1 - g, h, m], yrb.at[k, h, m], yfs.at[k, h, m], yfr.at[k, h, m], d_y)

    def project(j, b):
        r = order(z, j)
        rows = pl.ds(pl.multiple_of(W * r, W), W)

        @pl.loop(0, r + 1)
        def _(kc):
            t_sib(r, kc, b).wait_recv()
            t_fwd(r, kc, b).wait_recv()

        acc[...] = jnp.zeros_like(acc)

        @pl.loop(0, r + 1)
        def _(kc):
            t = tbuf[kc, b, rows, :]
            th = t.astype(bf16)
            tl = (t - th.astype(f32)).astype(bf16)
            ks = pl.ds(pl.multiple_of(W * kc, W), W)
            ch = chi[b, ks, :]
            acc[...] += (jnp.dot(th, ch, preferred_element_type=f32)
                         + jnp.dot(th, clo[b, ks, :], preferred_element_type=f32)
                         + jnp.dot(tl, ch, preferred_element_type=f32))

        full = acc[...]
        colbuf[z, r, W * b:W * (b + 1), :] = full.astype(bf16)
        pin(z, r, b).start()
        rowt[c, r, :, W * b:W * (b + 1)] = full.T.astype(bf16)

    def split(b):
        cc = cbuf[b]
        hi = cc.astype(bf16)
        chi[b] = hi
        clo[b] = (cc - hi.astype(f32)).astype(bf16)

    def near(m):
        def fn(r, b):
            px(0, c, r, b, m).wait_recv()
            px(2, xn, r, b, m).start()

            @pl.when(is_end)
            def _():
                rup(r, b, m).start()
        return fn

    def strip(r, b):
        pin(e, r, b).wait_recv()
        pfwd(e, r, b, 0).start()
        rowe[c, r, :, W * b:W * (b + 1)] = colbuf[e, r, W * b:W * (b + 1), :].astype(f32).T.astype(bf16)
        rshare(0, c, r, b, 0).start()
        rshare(0, c, r, b, 1).start()

    def both(fn, zz, i):
        r = order(zz, i)
        for b in range(nb):
            fn(r, b)

    def first(j):
        for b in range(nb):
            t_first(j, b)

    def get(j):
        for b in range(nb):
            t_second(j, b)
            project(j, b)

    def across(m):
        def fn(r, b):
            px(0, c, r, b, m).start()
            px(1, c, r, b, m).start()
        return fn

    def outward(r, b):
        @pl.when(is_mid)
        def _():
            pout(z, r, b).start()

    first(0)
    cload.wait()
    t_first(1, 0)
    split(0)
    t_first(1, 1)
    split(1)

    @pl.when(is_end)
    def _():
        get(0)

    first(2)

    @pl.when(is_mid)
    def _():
        get(0)

    get(1)
    first(3)

    @pl.when(is_mid)
    def _():
        both(strip, e, 0)

    get(2)
    for i in range(3):
        both(across(0), z, i)

    @pl.when(is_mid)
    def _():
        both(strip, e, 1)

    get(3)
    both(across(0), z, 3)
    for i in range(4):
        both(outward, z, i)
        both(across(1), z, i)

    def block(lhs, cp, ro, rn, s, lo, n):
        total = jnp.dot(lhs[cp, 0, ro:ro + rn, :], colbuf[s, 0, :, lo:lo + n], preferred_element_type=f32)
        for r in range(1, 4):
            total += jnp.dot(lhs[cp, r, ro:ro + rn, :], colbuf[s, r, :, lo:lo + n], preferred_element_type=f32)
        return total

    both_halves = (0, 1)

    def coded(lhs, p, s, halves, ms, ref, at):
        lo, n, ro, rn = H * halves[0], H * len(halves), H * ms[0], H * len(ms)

        def tile(i, top):
            t = block(lhs, 2 * p + i, ro, rn, s, lo, n)
            raw[i, 0:rn, 0:n] = t
            return jnp.maximum(top, jnp.max(jnp.abs(t), axis=0, keepdims=True))

        top = lax.fori_loop(0, 2, tile, jnp.full((1, n), LEAST, f32))
        scale = jnp.broadcast_to(1.0 / top, (16, n)).astype(bf16)
        factor = scale[0:1, :].astype(f32)

        @pl.loop(0, 2)
        def _(i):
            t = encode(raw[i, 0:rn, 0:n], factor)
            for q, h in enumerate(halves):
                for u, m in enumerate(ms):
                    ref[(*at, h, m, pl.ds(pl.multiple_of(H * i, H), H), slice(None))] = (
                        t[H * u:H * (u + 1), H * q:H * (q + 1)])

        for q, h in enumerate(halves):
            for m in ms:
                ref[(*at, h, m, slice(W, W + 16), slice(None))] = scale[:, H * q:H * (q + 1)]

    def read(ref, at, part):
        return decode(ref[(*at, part, slice(None))], ref[(*at, slice(W, W + 16), slice(None))].astype(f32)[0:1, :])

    def send(s, halves, ms):
        coded(rowt, 1 - g, s, halves, ms, sbuf, (s,))
        for h in halves:
            for m in ms:
                rs(s, h, m).start()

    def lend(k, s, p, halves, ms):
        coded(rowe, p, s, halves, ms, dsb, (k, p))
        for h in halves:
            for m in ms:
                dm(k, p, h, m).start()

    def keep(s, ms):
        cols, ro, rn = pl.ds(pl.multiple_of(W * s, W), W), H * ms[0], H * len(ms)

        @pl.loop(0, 2)
        def _(i):
            out[pl.ds(pl.multiple_of(W * i + ro, H), rn), cols] = block(rowt, 2 * g + i, ro, rn, s, 0, W)

    def work(s, p, ms):
        @pl.when(p == g)
        def _():
            keep(s, ms)

        @pl.when(p != g)
        def _():
            send(s, both_halves, ms)

    def parts(s):
        for h in (0, 1):
            cols = pl.ds(pl.multiple_of(W * s + H * h, H), H)
            for m in (0, 1):
                for i in (0, 1):
                    yield h, m, i, slice(W * i + H * m, W * i + H * (m + 1)), cols, slice(H * i, H * (i + 1))

    def finish(s):
        for h, m, i, rows, cols, part in parts(s):
            if i == 0:
                rs(s, h, m).wait_recv()
            out[rows, cols] = out[rows, cols] + read(rbuf, (s, h, m), part)

    def settle(k, s, hs):
        for h, m, i, rows, cols, part in parts(s):
            if h in hs:
                if i == 0:
                    yf(k, h, m).wait_recv()
                out[rows, cols] = read(drb, (k, g, h, m), part) + read(yrb, (k, h, m), part)

    def pass_on(k, p, h, m):
        dm(k, p, h, m).wait_recv()

        @pl.when(p != g)
        def _():
            yf(k, h, m).start()

    def every(fn):
        for r in range(4):
            for b in range(nb):
                fn(r, b)

    def sib_rows():
        for m in (0, 1):
            every(lambda r, b: px(1, sib, r, b, m).wait_recv())

    def far_rows(m):
        every(lambda r, b: px(2, xs, r, b, m).wait_recv())

    def lent_rows(route, col, ms):
        for m in ms:
            every(lambda r, b: rshare(route, col, r, b, m).wait_recv())

    @pl.when(is_mid)
    def _():
        def turn(m):
            def fn(r, b):
                rup(r, b, m).wait_recv()
                rshare(1, xn, r, b, m).start()
            return fn

        sib_rows()
        work(z, xp, both_halves)
        both(near(0), z, 0)
        both(near(0), z, 1)
        both(strip, e, 2)
        both(near(0), z, 2)
        both(strip, e, 3)
        for i in range(4):
            both(lambda r, b: pfwd(e, r, b, 1).start(), e, i)
        both(near(0), z, 3)
        work(e, xp, both_halves)
        far_rows(0)
        work(z, 1 - xp, (0,))
        work(e, 1 - xp, (0,))
        for i in range(4):
            both(lambda r, b: pin(o, r, b).wait_recv(), o, i)
        lent_rows(0, sib, both_halves)
        lend(0, o, xp, both_halves, both_halves)
        both(near(1), z, 0)
        both(near(1), z, 1)
        work(o, 1 - xp, (0,))
        for i in range(4):
            if i >= 2:
                both(near(1), z, i)
            both(turn(0), e, i)
        far_rows(1)
        for s in (z, e, o):
            work(s, 1 - xp, (1,))
        lent_rows(1, xs, (0,))
        lend(0, o, 1 - xp, both_halves, (0,))
        for i in range(4):
            both(lambda r, b: pfwd(f, r, b, 0).wait_recv(), f, i)
        lend(1, f, xp, (0,), both_halves)
        lend(1, f, 1 - xp, (0,), (0,))
        work(o, xp, both_halves)
        for i in range(4):
            both(turn(1), e, i)
        lent_rows(1, xs, (1,))
        lend(0, o, 1 - xp, both_halves, (1,))
        lend(1, f, 1 - xp, (0,), (1,))
        finish(z)
        finish(e)
        for i in range(4):
            both(lambda r, b: pfwd(f, r, b, 1).wait_recv(), f, i)
        lend(1, f, 1 - g, (1,), both_halves)
        lend(1, f, g, (1,), both_halves)
        send(f, both_halves, both_halves)
        keep(f, both_halves)
        finish(o)
        finish(f)

    @pl.when(is_end)
    def _():
        inner = 1 + z // 3
        both(near(0), z, 0)
        sib_rows()
        work(z, xp, both_halves)
        for i in range(1, 4):
            both(near(0), z, i)
        far_rows(0)
        work(z, 1 - xp, (0,))
        both(near(1), z, 0)
        both(near(1), z, 1)
        for i in range(4):
            both(lambda r, b: pout(inner, r, b).wait_recv(), inner, i)
        work(inner, 1 - xp, (0,))
        both(near(1), z, 2)
        both(near(1), z, 3)
        far_rows(1)
        work(z, 1 - xp, (1,))
        work(inner, 1 - xp, (1,))
        work(inner, xp, both_halves)

        def pass_both(k, p, hs, ms):
            for h in hs:
                for m in ms:
                    pass_on(k, p, h, m)

        pass_both(0, xp, both_halves, both_halves)
        pass_both(0, 1 - xp, both_halves, (0,))
        pass_both(1, xp, (0,), both_halves)
        pass_both(1, 1 - xp, (0,), (0,))
        finish(z)
        finish(inner)
        pass_both(0, 1 - xp, both_halves, (1,))
        pass_both(1, 1 - xp, (0,), (1,))
        settle(0, 3 - inner, both_halves)
        pass_both(1, 1 - g, (1,), both_halves)
        settle(1, 3 - z, (0,))
        pass_both(1, g, (1,), both_halves)
        settle(1, 3 - z, (1,))

    def sent(r, b):
        for kc in range(4):
            @pl.when(kc <= r)
            def _():
                @pl.when((r <= z) & (z < 3))
                def _():
                    t_up(r, kc, b).wait_send()

                @pl.when((r >= z) & (z > 0))
                def _():
                    t_dn(r, kc, b).wait_send()

                t_xn(r, kc, b).wait_send()
                t_sib(r, kc, b).wait_send()
                t_fwd(r, kc, b).wait_send()
        pin(z, r, b).wait_send()
        for m in (0, 1):
            px(0, c, r, b, m).wait_send()
            px(1, c, r, b, m).wait_send()
            px(2, xn, r, b, m).wait_send()

        @pl.when(is_mid)
        def _():
            pout(z, r, b).wait_send()
            for m in (0, 1):
                rshare(0, c, r, b, m).wait_send()
                rshare(1, xn, r, b, m).wait_send()
                pfwd(e, r, b, m).wait_send()

        @pl.when(is_end)
        def _():
            for m in (0, 1):
                rup(r, b, m).wait_send()

    @pl.loop(0, 4)
    def _(r):
        for b in range(nb):
            sent(r, b)

    for h in (0, 1):
        for m in (0, 1):
            rs(z, h, m).wait_send()
            rs(z + 1 - 2 * (z // 2), h, m).wait_send()

            @pl.when(is_mid)
            def _():
                rs(e, h, m).wait_send()
                rs(f, h, m).wait_send()
                for k in (0, 1):
                    dm(k, 0, h, m).wait_send()
                    dm(k, 1, h, m).wait_send()

            @pl.when(is_end)
            def _():
                yf(0, h, m).wait_send()
                yf(1, h, m).wait_send()


def single(nb, fac, piv, c_hbm, out, tbuf, cbuf, chi, clo, acc, colbuf, rowt, obuf,
           csem, tss, trs, pzs, pzr, phs, phr, pxs, pxr, osem):
    g, z, c = lax.axis_index("grp"), lax.axis_index("row"), lax.axis_index("col")
    sib = c + 1 - 2 * (c % 2)
    xn = (c + 2) % 4
    d_up, d_dn = (g, z + 1, c), (g, z - 1, c)
    d_xn, d_sib = (g, z, xn), (g, z, sib)
    piece = fac.shape[1]

    def order(zz, j):
        if j == 0:
            return zz
        if j == 1:
            return zz - 1 + 2 * ((3 - zz) // 3)
        if j == 2:
            return zz + 1 + (3 - zz) // 3 - 3 * (zz // 3)
        return 3 - 3 * (zz // 2)

    cload = pltpu.make_async_copy(c_hbm, cbuf, csem)
    cload.start()

    bar = pltpu.get_barrier_semaphore()

    def hello(dev):
        pl.semaphore_signal(bar, inc=1, device_id=dev, device_id_type=MESH)

    hello(d_xn)
    hello(d_sib)

    @pl.when(z < 3)
    def _():
        hello(d_up)

    @pl.when(z > 0)
    def _():
        hello(d_dn)

    for kc in range(4):
        @pl.when(kc <= z)
        def _():
            start = W * z + piece * c
            rows = start + lax.broadcasted_iota(jnp.int32, (piece, W), 0)
            cols = W * kc + lax.broadcasted_iota(jnp.int32, (piece, W), 1)
            for b in range(nb):
                diag = jnp.where(cols == rows, jnp.broadcast_to(piv[b:b + 1, :], (piece, W)), 0.0)
                tbuf[kc, b, pl.ds(pl.multiple_of(start, piece), piece), :] = jnp.where(
                    cols < rows, fac[b, :, W * kc:W * (kc + 1)], diag)

    pl.semaphore_wait(bar, 2 + (z + 3) // 4 + 1 - z // 3)

    def remote(ref, ss, rs, dev):
        return pltpu.make_async_remote_copy(
            src_ref=ref, dst_ref=ref, send_sem=ss, recv_sem=rs, device_id=dev, device_id_type=MESH)

    def tcopy(route, arrive, r, kc, col, dev):
        ref = tbuf.at[kc, :, pl.ds(pl.multiple_of(W * r + piece * col, piece), piece), :]
        return remote(ref, tss.at[route, r, kc], trs.at[arrive, r, kc], dev)

    def t_up(r, kc):
        return tcopy(0, 0, r, kc, c, d_up)

    def t_dn(r, kc):
        return tcopy(1, 0, r, kc, c, d_dn)

    def t_xn(r, kc):
        return tcopy(2, 1, r, kc, c, d_xn)

    def t_sib(r, kc):
        return tcopy(3, 2, r, kc, c, d_sib)

    def t_fwd(r, kc):
        return tcopy(4, 3, r, kc, xn, d_sib)

    def t_first(j):
        r = order(z, j)

        @pl.loop(0, r + 1)
        def _(kc):
            if j > 0:
                t_up(r, kc).wait_recv()

            @pl.when((r <= z) & (z < 3))
            def _():
                t_up(r, kc).start()

            @pl.when((r >= z) & (z > 0))
            def _():
                t_dn(r, kc).start()

            t_xn(r, kc).start()
            t_sib(r, kc).start()

    def t_second(j):
        r = order(z, j)

        @pl.loop(0, r + 1)
        def _(kc):
            t_xn(r, kc).wait_recv()
            t_fwd(r, kc).start()

    def pz(s, rg, up):
        return remote(colbuf.at[s, rg], pzs.at[0 if up else 1, s, rg], pzr.at[s, rg], d_up if up else d_dn)

    def px(route, col, rg):
        return remote(rowt.at[col, rg], pxs.at[route, rg], pxr.at[route, rg], d_xn if route == 0 else d_sib)

    def project(j):
        r = order(z, j)

        @pl.loop(0, r + 1)
        def _(kc):
            t_sib(r, kc).wait_recv()
            t_fwd(r, kc).wait_recv()

        rows = pl.ds(pl.multiple_of(W * r, W), W)
        for b in range(nb):
            acc[...] = jnp.zeros_like(acc)

            @pl.loop(0, r + 1)
            def _(kc):
                t = tbuf[kc, b, rows, :]
                th = t.astype(bf16)
                tl = (t - th.astype(f32)).astype(bf16)
                ks = pl.ds(pl.multiple_of(W * kc, W), W)
                ch = chi[b, ks, :]
                acc[...] += (jnp.dot(th, ch, preferred_element_type=f32)
                             + jnp.dot(th, clo[b, ks, :], preferred_element_type=f32)
                             + jnp.dot(tl, ch, preferred_element_type=f32))

            full = acc[...]
            colbuf[z, r, W * b:W * (b + 1), :] = full.astype(bf16)
            rowt[c, r, :, W * b:W * (b + 1)] = full.T.astype(bf16)

        @pl.when(z < 3)
        def _():
            pz(z, r, True).start()

        @pl.when(z > 0)
        def _():
            pz(z, r, False).start()

        px(0, c, r).start()
        px(1, c, r).start()

    t_first(0)
    cload.wait()
    for b in range(nb):
        cc = cbuf[b]
        hi = cc.astype(bf16)
        chi[b] = hi
        clo[b] = (cc - hi.astype(f32)).astype(bf16)
    t_first(1)
    t_first(2)
    t_second(0)
    project(0)
    t_first(3)
    t_second(1)
    project(1)
    t_second(2)
    project(2)
    t_second(3)
    project(3)

    H = W // 2

    def block(cp, s, lo, n):
        total = jnp.dot(rowt[cp, 0], colbuf[s, 0, :, lo:lo + n], preferred_element_type=f32)
        for rg in range(1, 4):
            total += jnp.dot(rowt[cp, rg], colbuf[s, rg, :, lo:lo + n], preferred_element_type=f32)
        return total

    def emit(s, h):
        cols = pl.ds(pl.multiple_of(W * s + H * h, H), H)
        return pltpu.make_async_copy(obuf.at[:, cols], out.at[:, cols], osem.at[s, h])

    def gram(s, halves):
        lo, n = H * halves[0], H * len(halves)
        cols = pl.ds(pl.multiple_of(W * s + lo, H), n)
        @pl.loop(0, 4)
        def _(i):
            obuf[pl.ds(pl.multiple_of(W * i, W), W), cols] = block(i, s, lo, n)

    def finish(s):
        for h in (0, 1):
            emit(s, h).start()

    def ph(s, rg, h, up):
        return remote(colbuf.at[s, rg, :, H * h:H * (h + 1)], phs.at[rg, h], phr.at[rg, h], d_up if up else d_dn)

    def near(i):
        lo, hi = z - 1, z + 1

        @pl.when(lo >= 0)
        def _():
            rg = order(lo, i)
            pz(lo, rg, True).wait_recv()

            @pl.when(z < 3)
            def _():
                pz(lo, rg, True).start()

        @pl.when(hi <= 3)
        def _():
            rg = order(hi, i)
            pz(hi, rg, False).wait_recv()

            @pl.when(z > 0)
            def _():
                pz(hi, rg, False).start()

    def second(s, up):
        for i in range(4):
            pz(s, order(s, i), up).wait_recv()

        @pl.when((z == 1) | (z == 2))
        def _():
            for h in (0, 1):
                for rg in range(4):
                    ph(s, rg, h, up).start()

        gram(s, (0, 1))

    def third(s, up):
        for h in (0, 1):
            for rg in range(4):
                ph(s, rg, h, up).wait_recv()
            gram(s, (h,))

    def each(d, fn):
        @pl.when(z - d >= 0)
        def _():
            fn(z - d, True)

        @pl.when(z + d <= 3)
        def _():
            fn(z + d, False)

    for i in range(4):
        near(i)
        r = order(z, i)
        px(0, c, r).wait_recv()
        px(2, xn, r).start()
    for i in range(4):
        px(1, c, i).wait_recv()
        px(2, c, i).wait_recv()
    gram(z, (0, 1))
    each(1, lambda s, up: gram(s, (0, 1)))
    each(2, second)
    finish(z)
    each(1, lambda s, up: finish(s))
    each(3, third)
    each(2, lambda s, up: finish(s))
    each(3, lambda s, up: finish(s))

    for r in range(4):
        for kc in range(r + 1):
            @pl.when((r <= z) & (z < 3))
            def _():
                t_up(r, kc).wait_send()

            @pl.when((r >= z) & (z > 0))
            def _():
                t_dn(r, kc).wait_send()

            t_xn(r, kc).wait_send()
            t_sib(r, kc).wait_send()
            t_fwd(r, kc).wait_send()
        for s in range(4):
            @pl.when((s <= z) & (z < 3) & (z - s < 2))
            def _():
                pz(s, r, True).wait_send()

            @pl.when((s >= z) & (z > 0) & (s - z < 2))
            def _():
                pz(s, r, False).wait_send()

        px(0, c, r).wait_send()
        px(1, c, r).wait_send()
        px(2, xn, r).wait_send()
        for h in (0, 1):
            @pl.when((z == 1) | (z == 2))
            def _():
                ph(3, r, h, False).wait_send()

            emit(r, h).wait()


LIMIT = 204


def body(groups, factor, pivots, constraints):
    nb, piece, order_m = factor.shape
    strip = constraints.shape[2]
    assert strip == W and order_m == 4 * W and piece * 4 == W
    dma = pltpu.SemaphoreType.DMA
    wide = [
        pltpu.VMEM((4, nb, 4 * W, W), f32),
        pltpu.VMEM((nb, 4 * W, W), f32),
        pltpu.VMEM((nb, 4 * W, W), bf16),
        pltpu.VMEM((nb, 4 * W, W), bf16),
        pltpu.VMEM((W, W), f32),
    ]
    vmem, anywhere = pl.BlockSpec(memory_space=pltpu.VMEM), pl.BlockSpec(memory_space=pl.ANY)
    if groups == 2:
        kernel, rows_out, limit = paired, 2 * W, LIMIT
        in_specs, out_specs = [vmem, vmem, anywhere], vmem
        scratch = wide + [
            pltpu.VMEM((2, W, W), f32),
            pltpu.VMEM((4, 4, nb * W, W), bf16),
            pltpu.VMEM((4, 4, W, nb * W), bf16),
            pltpu.VMEM((4, 4, W, nb * W), bf16),
            pltpu.VMEM((4, 2, 2, W + 16, H), bf16),
            pltpu.VMEM((4, 2, 2, W + 16, H), bf16),
            pltpu.VMEM((2, 2, 2, 2, W + 16, H), bf16),
            pltpu.VMEM((2, 2, 2, 2, W + 16, H), bf16),
            pltpu.VMEM((2, 2, 2, W + 16, H), bf16),
            dma,
            dma((5, 4, 4, nb)),
            dma((4, 4, 4, nb)),
            dma((4, nb)),
            dma((4, 4, nb)),
            dma((4, nb)),
            dma((4, nb)),
            dma((4, nb, 2)),
            dma((4, nb, 2)),
            dma((3, 4, nb, 2)),
            dma((3, 4, nb, 2)),
            dma((4, nb, 2)),
            dma((4, nb, 2)),
            dma((2, 4, nb, 2)),
            dma((2, 4, nb, 2)),
            dma((4, 2, 2)),
            dma((4, 2, 2)),
            dma((2, 2, 2, 2)),
            dma((2, 2, 2, 2)),
            dma((2, 2, 2)),
            dma((2, 2, 2)),
        ]
    else:
        kernel, rows_out, limit = single, 4 * W, 208
        pivots = jnp.tile(pivots, (1, 4))
        in_specs, out_specs = [vmem, vmem, anywhere], anywhere
        scratch = wide + [
            pltpu.VMEM((4, 4, nb * W, W), bf16),
            pltpu.VMEM((4, 4, W, nb * W), bf16),
            pltpu.VMEM((rows_out, 4 * W), f32),
            dma,
            dma((5, 4, 4)),
            dma((4, 4, 4)),
            dma((2, 4, 4)),
            dma((4, 4)),
            dma((4, 2)),
            dma((4, 2)),
            dma((3, 4)),
            dma((3, 4)),
            dma((4, 2)),
        ]
    result = pl.pallas_call(
        functools.partial(kernel, nb),
        out_shape=jax.ShapeDtypeStruct((rows_out, 4 * W), f32),
        in_specs=in_specs,
        out_specs=out_specs,
        scratch_shapes=scratch,
        compiler_params=pltpu.CompilerParams(
            collective_id=0, has_side_effects=True, vmem_limit_bytes=limit << 18),
    )(factor, pivots, constraints)
    if groups != 2:
        result = lax.psum_scatter(result, "grp", scatter_dimension=0, tiled=True)
    return result[None]


def solution(mesh):
    in_specs = (
        P("grp", ("row", "col"), None),
        P("grp", ("row", "col")),
        P("grp", None, ("col", "row")),
    )
    return jax.shard_map(
        functools.partial(body, mesh.shape["grp"]), mesh=mesh, in_specs=in_specs,
        out_specs=P("row", "grp", "col"), check_vma=False)
```

```python
import functools
import jax
import jax.numpy as jnp
from jax import lax
from jax.experimental import pallas as pl
from jax.experimental.pallas import tpu as pltpu
from jax.sharding import PartitionSpec as P

MESH = pl.DeviceIdType.MESH
f32 = jnp.float32
bf16 = jnp.bfloat16
W = 256


H = W // 2
TOP = 2.0 ** 30
LEAST = 1e-25


def encode(t, scale):
    a = t * (scale * TOP)
    return (a * jnp.abs(a) * (a * a)).astype(bf16)


def decode(w, scale):
    a = w.astype(f32)
    root = jnp.sqrt(jnp.sqrt(jnp.abs(a))) * (1.0 / (scale * TOP))
    return jnp.where(a < 0, -root, root)


def order(zz, j):
    if j == 0:
        return zz
    if j == 1:
        return zz - 1 + 2 * ((3 - zz) // 3)
    if j == 2:
        return zz + 1 + (3 - zz) // 3 - 3 * (zz // 3)
    return 3 - 3 * (zz // 2)


def paired(nb, fac, piv, c_hbm, out, tbuf, cbuf, chi, clo, acc, raw, colbuf, rowt, rowe, sbuf, rbuf,
           dsb, drb, yrb, csem, tss, trs, pis, pir, pos, por, pfs, pfr, pxs, pxr, res, rer, rcs, rcr, rss, rsr,
           dms, dmr, yfs, yfr):
    g, z, c = lax.axis_index("grp"), lax.axis_index("row"), lax.axis_index("col")
    sib = c + 1 - 2 * (c % 2)
    xn = (c + 2) % 4
    xs = (sib + 2) % 4
    xp = c // 2
    d_up, d_dn = (g, z + 1, c), (g, z - 1, c)
    d_xn, d_sib = (g, z, xn), (g, z, sib)
    d_y = (1 - g, z, c)
    e = 3 * (z // 2)
    f = 3 - e
    o = 3 - z
    d_in = (g, z + 1 - 2 * (z // 2), c)
    d_end = (g, e, c)
    is_mid = (z == 1) | (z == 2)
    is_end = (z == 0) | (z == 3)
    piece = fac.shape[1]

    cload = pltpu.make_async_copy(c_hbm, cbuf, csem)
    cload.start()

    bar = pltpu.get_barrier_semaphore()

    def hello(dev):
        pl.semaphore_signal(bar, inc=1, device_id=dev, device_id_type=MESH)

    hello(d_xn)
    hello(d_sib)
    hello(d_y)

    @pl.when(z < 3)
    def _():
        hello(d_up)

    @pl.when(z > 0)
    def _():
        hello(d_dn)

    for kc in range(4):
        @pl.when(kc <= z)
        def _():
            start = W * z + piece * c
            rows = start + lax.broadcasted_iota(jnp.int32, (piece, W), 0)
            cols = W * kc + lax.broadcasted_iota(jnp.int32, (piece, W), 1)
            for b in range(nb):
                own = jnp.concatenate([piv[b:b + 1, :]] * (W // piece), axis=1)
                diag = jnp.where(cols == rows, jnp.broadcast_to(own, (piece, W)), 0.0)
                tbuf[kc, b, pl.ds(pl.multiple_of(start, piece), piece), :] = jnp.where(
                    cols < rows, fac[b, :, W * kc:W * (kc + 1)], diag)

    pl.semaphore_wait(bar, 3 + (z + 3) // 4 + 1 - z // 3)

    def remote(src, dst, ss, rs, dev):
        return pltpu.make_async_remote_copy(
            src_ref=src, dst_ref=dst, send_sem=ss, recv_sem=rs, device_id=dev, device_id_type=MESH)

    def tcopy(route, arrive, r, kc, b, col, dev):
        ref = tbuf.at[kc, b, pl.ds(pl.multiple_of(W * r + piece * col, piece), piece), :]
        return remote(ref, ref, tss.at[route, r, kc, b], trs.at[arrive, r, kc, b], dev)

    def t_up(r, kc, b):
        return tcopy(0, 0, r, kc, b, c, d_up)

    def t_dn(r, kc, b):
        return tcopy(1, 0, r, kc, b, c, d_dn)

    def t_xn(r, kc, b):
        return tcopy(2, 1, r, kc, b, c, d_xn)

    def t_sib(r, kc, b):
        return tcopy(3, 2, r, kc, b, c, d_sib)

    def t_fwd(r, kc, b):
        return tcopy(4, 3, r, kc, b, xn, d_sib)

    def t_first(j, b):
        r = order(z, j)

        @pl.loop(0, r + 1)
        def _(kc):
            if j > 0:
                t_up(r, kc, b).wait_recv()

            @pl.when((r <= z) & (z < 3))
            def _():
                t_up(r, kc, b).start()

            @pl.when((r >= z) & (z > 0))
            def _():
                t_dn(r, kc, b).start()

            t_xn(r, kc, b).start()
            t_sib(r, kc, b).start()

    def t_second(j, b):
        r = order(z, j)

        @pl.loop(0, r + 1)
        def _(kc):
            t_xn(r, kc, b).wait_recv()
            t_fwd(r, kc, b).start()

    def pin(s, r, b):
        ref = colbuf.at[s, r, W * b:W * (b + 1), :]
        return remote(ref, ref, pis.at[r, b], pir.at[s, r, b], d_in)

    def pout(s, r, b):
        ref = colbuf.at[s, r, W * b:W * (b + 1), :]
        return remote(ref, ref, pos.at[r, b], por.at[r, b], d_end)

    def pfwd(s, r, b, h):
        ref = colbuf.at[s, r, W * b:W * (b + 1), H * h:H * (h + 1)]
        return remote(ref, ref, pfs.at[r, b, h], pfr.at[r, b, h], d_in)

    def px(route, col, r, b, m):
        ref = rowt.at[col, r, H * m:H * (m + 1), W * b:W * (b + 1)]
        return remote(ref, ref, pxs.at[route, r, b, m], pxr.at[route, r, b, m], d_xn if route == 0 else d_sib)

    def rup(r, b, m):
        part = (xn, r, slice(H * m, H * (m + 1)), slice(W * b, W * (b + 1)))
        return remote(rowt.at[part], rowe.at[part], res.at[r, b, m], rer.at[r, b, m], d_in)

    def rshare(route, col, r, b, m):
        ref = rowe.at[col, r, H * m:H * (m + 1), W * b:W * (b + 1)]
        return remote(ref, ref, rcs.at[route, r, b, m], rcr.at[route, r, b, m], d_sib)

    def rs(s, h, m):
        return remote(sbuf.at[s, h, m], rbuf.at[s, h, m], rss.at[s, h, m], rsr.at[s, h, m], d_y)

    def dm(k, p, h, m):
        return remote(dsb.at[k, p, h, m], drb.at[k, p, h, m], dms.at[k, p, h, m], dmr.at[k, p, h, m], d_end)

    def yf(k, h, m):
        return remote(drb.at[k, 1 - g, h, m], yrb.at[k, h, m], yfs.at[k, h, m], yfr.at[k, h, m], d_y)

    def project(j, b):
        r = order(z, j)
        rows = pl.ds(pl.multiple_of(W * r, W), W)

        @pl.loop(0, r + 1)
        def _(kc):
            t_sib(r, kc, b).wait_recv()
            t_fwd(r, kc, b).wait_recv()

        acc[...] = jnp.zeros_like(acc)

        @pl.loop(0, r + 1)
        def _(kc):
            t = tbuf[kc, b, rows, :]
            th = t.astype(bf16)
            tl = (t - th.astype(f32)).astype(bf16)
            ks = pl.ds(pl.multiple_of(W * kc, W), W)
            ch = chi[b, ks, :]
            acc[...] += (jnp.dot(th, ch, preferred_element_type=f32)
                         + jnp.dot(th, clo[b, ks, :], preferred_element_type=f32)
                         + jnp.dot(tl, ch, preferred_element_type=f32))

        full = acc[...]
        colbuf[z, r, W * b:W * (b + 1), :] = full.astype(bf16)
        pin(z, r, b).start()
        rowt[c, r, :, W * b:W * (b + 1)] = full.T.astype(bf16)

    def split(b):
        cc = cbuf[b]
        hi = cc.astype(bf16)
        chi[b] = hi
        clo[b] = (cc - hi.astype(f32)).astype(bf16)

    def near(m):
        def fn(r, b):
            px(0, c, r, b, m).wait_recv()
            px(2, xn, r, b, m).start()

            @pl.when(is_end)
            def _():
                rup(r, b, m).start()
        return fn

    def strip(r, b):
        pin(e, r, b).wait_recv()
        pfwd(e, r, b, 0).start()
        rowe[c, r, :, W * b:W * (b + 1)] = colbuf[e, r, W * b:W * (b + 1), :].astype(f32).T.astype(bf16)
        rshare(0, c, r, b, 0).start()
        rshare(0, c, r, b, 1).start()

    def both(fn, zz, i):
        r = order(zz, i)
        for b in range(nb):
            fn(r, b)

    def first(j):
        for b in range(nb):
            t_first(j, b)

    def get(j):
        for b in range(nb):
            t_second(j, b)
            project(j, b)

    def across(m):
        def fn(r, b):
            px(0, c, r, b, m).start()
            px(1, c, r, b, m).start()
        return fn

    def outward(r, b):
        @pl.when(is_mid)
        def _():
            pout(z, r, b).start()

    first(0)
    cload.wait()
    t_first(1, 0)
    split(0)
    t_first(1, 1)
    split(1)

    @pl.when(is_end)
    def _():
        get(0)

    first(2)

    @pl.when(is_mid)
    def _():
        get(0)

    get(1)
    first(3)

    @pl.when(is_mid)
    def _():
        both(strip, e, 0)

    get(2)
    for i in range(3):
        both(across(0), z, i)

    @pl.when(is_mid)
    def _():
        both(strip, e, 1)

    get(3)
    both(across(0), z, 3)
    for i in range(4):
        both(outward, z, i)
        both(across(1), z, i)

    def block(lhs, cp, ro, rn, s, lo, n):
        total = jnp.dot(lhs[cp, 0, ro:ro + rn, :], colbuf[s, 0, :, lo:lo + n], preferred_element_type=f32)
        for r in range(1, 4):
            total += jnp.dot(lhs[cp, r, ro:ro + rn, :], colbuf[s, r, :, lo:lo + n], preferred_element_type=f32)
        return total

    both_halves = (0, 1)

    def coded(lhs, p, s, halves, ms, ref, at):
        lo, n, ro, rn = H * halves[0], H * len(halves), H * ms[0], H * len(ms)

        def tile(i, top):
            t = block(lhs, 2 * p + i, ro, rn, s, lo, n)
            raw[i, 0:rn, 0:n] = t
            return jnp.maximum(top, jnp.max(jnp.abs(t), axis=0, keepdims=True))

        top = lax.fori_loop(0, 2, tile, jnp.full((1, n), LEAST, f32))
        scale = jnp.broadcast_to(1.0 / top, (16, n)).astype(bf16)
        factor = scale[0:1, :].astype(f32)

        @pl.loop(0, 2)
        def _(i):
            t = encode(raw[i, 0:rn, 0:n], factor)
            for q, h in enumerate(halves):
                for u, m in enumerate(ms):
                    ref[(*at, h, m, pl.ds(pl.multiple_of(H * i, H), H), slice(None))] = (
                        t[H * u:H * (u + 1), H * q:H * (q + 1)])

        for q, h in enumerate(halves):
            for m in ms:
                ref[(*at, h, m, slice(W, W + 16), slice(None))] = scale[:, H * q:H * (q + 1)]

    def read(ref, at, part):
        return decode(ref[(*at, part, slice(None))], ref[(*at, slice(W, W + 16), slice(None))].astype(f32)[0:1, :])

    def send(s, halves, ms):
        coded(rowt, 1 - g, s, halves, ms, sbuf, (s,))
        for h in halves:
            for m in ms:
                rs(s, h, m).start()

    def lend(k, s, p, halves, ms):
        coded(rowe, p, s, halves, ms, dsb, (k, p))
        for h in halves:
            for m in ms:
                dm(k, p, h, m).start()

    def keep(s, ms):
        cols, ro, rn = pl.ds(pl.multiple_of(W * s, W), W), H * ms[0], H * len(ms)

        @pl.loop(0, 2)
        def _(i):
            out[pl.ds(pl.multiple_of(W * i + ro, H), rn), cols] = block(rowt, 2 * g + i, ro, rn, s, 0, W)

    def work(s, p, ms):
        @pl.when(p == g)
        def _():
            keep(s, ms)

        @pl.when(p != g)
        def _():
            send(s, both_halves, ms)

    def parts(s):
        for h in (0, 1):
            cols = pl.ds(pl.multiple_of(W * s + H * h, H), H)
            for m in (0, 1):
                for i in (0, 1):
                    yield h, m, i, slice(W * i + H * m, W * i + H * (m + 1)), cols, slice(H * i, H * (i + 1))

    def finish(s):
        for h, m, i, rows, cols, part in parts(s):
            if i == 0:
                rs(s, h, m).wait_recv()
            out[rows, cols] = out[rows, cols] + read(rbuf, (s, h, m), part)

    def settle(k, s, hs):
        for h, m, i, rows, cols, part in parts(s):
            if h in hs:
                if i == 0:
                    yf(k, h, m).wait_recv()
                out[rows, cols] = read(drb, (k, g, h, m), part) + read(yrb, (k, h, m), part)

    def pass_on(k, p, h, m):
        dm(k, p, h, m).wait_recv()

        @pl.when(p != g)
        def _():
            yf(k, h, m).start()

    def every(fn):
        for r in range(4):
            for b in range(nb):
                fn(r, b)

    def sib_rows():
        for m in (0, 1):
            every(lambda r, b: px(1, sib, r, b, m).wait_recv())

    def far_rows(m):
        every(lambda r, b: px(2, xs, r, b, m).wait_recv())

    def lent_rows(route, col, ms):
        for m in ms:
            every(lambda r, b: rshare(route, col, r, b, m).wait_recv())

    @pl.when(is_mid)
    def _():
        def turn(m):
            def fn(r, b):
                rup(r, b, m).wait_recv()
                rshare(1, xn, r, b, m).start()
            return fn

        sib_rows()
        work(z, xp, both_halves)
        both(near(0), z, 0)
        both(near(0), z, 1)
        both(strip, e, 2)
        both(near(0), z, 2)
        both(strip, e, 3)
        for i in range(4):
            both(lambda r, b: pfwd(e, r, b, 1).start(), e, i)
        both(near(0), z, 3)
        work(e, xp, both_halves)
        far_rows(0)
        work(z, 1 - xp, (0,))
        work(e, 1 - xp, (0,))
        for i in range(4):
            both(lambda r, b: pin(o, r, b).wait_recv(), o, i)
        lent_rows(0, sib, both_halves)
        lend(0, o, xp, both_halves, both_halves)
        both(near(1), z, 0)
        both(near(1), z, 1)
        work(o, 1 - xp, (0,))
        for i in range(4):
            if i >= 2:
                both(near(1), z, i)
            both(turn(0), e, i)
        far_rows(1)
        for s in (z, e, o):
            work(s, 1 - xp, (1,))
        lent_rows(1, xs, (0,))
        lend(0, o, 1 - xp, both_halves, (0,))
        for i in range(4):
            both(lambda r, b: pfwd(f, r, b, 0).wait_recv(), f, i)
        lend(1, f, xp, (0,), both_halves)
        lend(1, f, 1 - xp, (0,), (0,))
        work(o, xp, both_halves)
        for i in range(4):
            both(turn(1), e, i)
        lent_rows(1, xs, (1,))
        lend(0, o, 1 - xp, both_halves, (1,))
        lend(1, f, 1 - xp, (0,), (1,))
        finish(z)
        finish(e)
        for i in range(4):
            both(lambda r, b: pfwd(f, r, b, 1).wait_recv(), f, i)
        lend(1, f, 1 - g, (1,), both_halves)
        lend(1, f, g, (1,), both_halves)
        send(f, both_halves, both_halves)
        keep(f, both_halves)
        finish(o)
        finish(f)

    @pl.when(is_end)
    def _():
        inner = 1 + z // 3
        both(near(0), z, 0)
        sib_rows()
        work(z, xp, both_halves)
        for i in range(1, 4):
            both(near(0), z, i)
        far_rows(0)
        work(z, 1 - xp, (0,))
        both(near(1), z, 0)
        both(near(1), z, 1)
        for i in range(4):
            both(lambda r, b: pout(inner, r, b).wait_recv(), inner, i)
        work(inner, 1 - xp, (0,))
        both(near(1), z, 2)
        both(near(1), z, 3)
        far_rows(1)
        work(z, 1 - xp, (1,))
        work(inner, 1 - xp, (1,))
        work(inner, xp, both_halves)

        def pass_both(k, p, hs, ms):
            for h in hs:
                for m in ms:
                    pass_on(k, p, h, m)

        pass_both(0, xp, both_halves, both_halves)
        pass_both(0, 1 - xp, both_halves, (0,))
        pass_both(1, xp, (0,), both_halves)
        pass_both(1, 1 - xp, (0,), (0,))
        pass_both(0, 1 - xp, both_halves, (1,))
        pass_both(1, 1 - xp, (0,), (1,))
        finish(z)
        finish(inner)
        pass_both(1, 1 - g, (1,), both_halves)
        settle(0, 3 - inner, both_halves)
        settle(1, 3 - z, (0,))
        pass_both(1, g, (1,), both_halves)
        settle(1, 3 - z, (1,))

    def sent(r, b):
        for kc in range(4):
            @pl.when(kc <= r)
            def _():
                @pl.when((r <= z) & (z < 3))
                def _():
                    t_up(r, kc, b).wait_send()

                @pl.when((r >= z) & (z > 0))
                def _():
                    t_dn(r, kc, b).wait_send()

                t_xn(r, kc, b).wait_send()
                t_sib(r, kc, b).wait_send()
                t_fwd(r, kc, b).wait_send()
        pin(z, r, b).wait_send()
        for m in (0, 1):
            px(0, c, r, b, m).wait_send()
            px(1, c, r, b, m).wait_send()
            px(2, xn, r, b, m).wait_send()

        @pl.when(is_mid)
        def _():
            pout(z, r, b).wait_send()
            for m in (0, 1):
                rshare(0, c, r, b, m).wait_send()
                rshare(1, xn, r, b, m).wait_send()
                pfwd(e, r, b, m).wait_send()

        @pl.when(is_end)
        def _():
            for m in (0, 1):
                rup(r, b, m).wait_send()

    @pl.loop(0, 4)
    def _(r):
        for b in range(nb):
            sent(r, b)

    for h in (0, 1):
        for m in (0, 1):
            rs(z, h, m).wait_send()
            rs(z + 1 - 2 * (z // 2), h, m).wait_send()

            @pl.when(is_mid)
            def _():
                rs(e, h, m).wait_send()
                rs(f, h, m).wait_send()
                for k in (0, 1):
                    dm(k, 0, h, m).wait_send()
                    dm(k, 1, h, m).wait_send()

            @pl.when(is_end)
            def _():
                yf(0, h, m).wait_send()
                yf(1, h, m).wait_send()


def single(nb, fac, piv, c_hbm, out, tbuf, cbuf, chi, clo, acc, colbuf, rowt, obuf,
           csem, tss, trs, pzs, pzr, phs, phr, pxs, pxr, osem):
    g, z, c = lax.axis_index("grp"), lax.axis_index("row"), lax.axis_index("col")
    sib = c + 1 - 2 * (c % 2)
    xn = (c + 2) % 4
    d_up, d_dn = (g, z + 1, c), (g, z - 1, c)
    d_xn, d_sib = (g, z, xn), (g, z, sib)
    piece = fac.shape[1]

    def order(zz, j):
        if j == 0:
            return zz
        if j == 1:
            return zz - 1 + 2 * ((3 - zz) // 3)
        if j == 2:
            return zz + 1 + (3 - zz) // 3 - 3 * (zz // 3)
        return 3 - 3 * (zz // 2)

    cload = pltpu.make_async_copy(c_hbm, cbuf, csem)
    cload.start()

    bar = pltpu.get_barrier_semaphore()

    def hello(dev):
        pl.semaphore_signal(bar, inc=1, device_id=dev, device_id_type=MESH)

    hello(d_xn)
    hello(d_sib)

    @pl.when(z < 3)
    def _():
        hello(d_up)

    @pl.when(z > 0)
    def _():
        hello(d_dn)

    for kc in range(4):
        @pl.when(kc <= z)
        def _():
            start = W * z + piece * c
            rows = start + lax.broadcasted_iota(jnp.int32, (piece, W), 0)
            cols = W * kc + lax.broadcasted_iota(jnp.int32, (piece, W), 1)
            for b in range(nb):
                diag = jnp.where(cols == rows, jnp.broadcast_to(piv[b:b + 1, :], (piece, W)), 0.0)
                tbuf[kc, b, pl.ds(pl.multiple_of(start, piece), piece), :] = jnp.where(
                    cols < rows, fac[b, :, W * kc:W * (kc + 1)], diag)

    pl.semaphore_wait(bar, 2 + (z + 3) // 4 + 1 - z // 3)

    def remote(ref, ss, rs, dev):
        return pltpu.make_async_remote_copy(
            src_ref=ref, dst_ref=ref, send_sem=ss, recv_sem=rs, device_id=dev, device_id_type=MESH)

    def tcopy(route, arrive, r, kc, col, dev):
        ref = tbuf.at[kc, :, pl.ds(pl.multiple_of(W * r + piece * col, piece), piece), :]
        return remote(ref, tss.at[route, r, kc], trs.at[arrive, r, kc], dev)

    def t_up(r, kc):
        return tcopy(0, 0, r, kc, c, d_up)

    def t_dn(r, kc):
        return tcopy(1, 0, r, kc, c, d_dn)

    def t_xn(r, kc):
        return tcopy(2, 1, r, kc, c, d_xn)

    def t_sib(r, kc):
        return tcopy(3, 2, r, kc, c, d_sib)

    def t_fwd(r, kc):
        return tcopy(4, 3, r, kc, xn, d_sib)

    def t_first(j):
        r = order(z, j)

        @pl.loop(0, r + 1)
        def _(kc):
            if j > 0:
                t_up(r, kc).wait_recv()

            @pl.when((r <= z) & (z < 3))
            def _():
                t_up(r, kc).start()

            @pl.when((r >= z) & (z > 0))
            def _():
                t_dn(r, kc).start()

            t_xn(r, kc).start()
            t_sib(r, kc).start()

    def t_second(j):
        r = order(z, j)

        @pl.loop(0, r + 1)
        def _(kc):
            t_xn(r, kc).wait_recv()
            t_fwd(r, kc).start()

    def pz(s, rg, up):
        return remote(colbuf.at[s, rg], pzs.at[0 if up else 1, s, rg], pzr.at[s, rg], d_up if up else d_dn)

    def px(route, col, rg):
        return remote(rowt.at[col, rg], pxs.at[route, rg], pxr.at[route, rg], d_xn if route == 0 else d_sib)

    def project(j):
        r = order(z, j)

        @pl.loop(0, r + 1)
        def _(kc):
            t_sib(r, kc).wait_recv()
            t_fwd(r, kc).wait_recv()

        rows = pl.ds(pl.multiple_of(W * r, W), W)
        for b in range(nb):
            acc[...] = jnp.zeros_like(acc)

            @pl.loop(0, r + 1)
            def _(kc):
                t = tbuf[kc, b, rows, :]
                th = t.astype(bf16)
                tl = (t - th.astype(f32)).astype(bf16)
                ks = pl.ds(pl.multiple_of(W * kc, W), W)
                ch = chi[b, ks, :]
                acc[...] += (jnp.dot(th, ch, preferred_element_type=f32)
                             + jnp.dot(th, clo[b, ks, :], preferred_element_type=f32)
                             + jnp.dot(tl, ch, preferred_element_type=f32))

            full = acc[...]
            colbuf[z, r, W * b:W * (b + 1), :] = full.astype(bf16)
            rowt[c, r, :, W * b:W * (b + 1)] = full.T.astype(bf16)

        @pl.when(z < 3)
        def _():
            pz(z, r, True).start()

        @pl.when(z > 0)
        def _():
            pz(z, r, False).start()

        px(0, c, r).start()
        px(1, c, r).start()

    t_first(0)
    cload.wait()
    for b in range(nb):
        cc = cbuf[b]
        hi = cc.astype(bf16)
        chi[b] = hi
        clo[b] = (cc - hi.astype(f32)).astype(bf16)
    t_first(1)
    t_first(2)
    t_second(0)
    project(0)
    t_first(3)
    t_second(1)
    project(1)
    t_second(2)
    project(2)
    t_second(3)
    project(3)

    H = W // 2

    def block(cp, s, lo, n):
        total = jnp.dot(rowt[cp, 0], colbuf[s, 0, :, lo:lo + n], preferred_element_type=f32)
        for rg in range(1, 4):
            total += jnp.dot(rowt[cp, rg], colbuf[s, rg, :, lo:lo + n], preferred_element_type=f32)
        return total

    def emit(s, h):
        cols = pl.ds(pl.multiple_of(W * s + H * h, H), H)
        return pltpu.make_async_copy(obuf.at[:, cols], out.at[:, cols], osem.at[s, h])

    def gram(s, halves):
        lo, n = H * halves[0], H * len(halves)
        cols = pl.ds(pl.multiple_of(W * s + lo, H), n)
        @pl.loop(0, 4)
        def _(i):
            obuf[pl.ds(pl.multiple_of(W * i, W), W), cols] = block(i, s, lo, n)

    def finish(s):
        for h in (0, 1):
            emit(s, h).start()

    def ph(s, rg, h, up):
        return remote(colbuf.at[s, rg, :, H * h:H * (h + 1)], phs.at[rg, h], phr.at[rg, h], d_up if up else d_dn)

    def near(i):
        lo, hi = z - 1, z + 1

        @pl.when(lo >= 0)
        def _():
            rg = order(lo, i)
            pz(lo, rg, True).wait_recv()

            @pl.when(z < 3)
            def _():
                pz(lo, rg, True).start()

        @pl.when(hi <= 3)
        def _():
            rg = order(hi, i)
            pz(hi, rg, False).wait_recv()

            @pl.when(z > 0)
            def _():
                pz(hi, rg, False).start()

    def second(s, up):
        for i in range(4):
            pz(s, order(s, i), up).wait_recv()

        @pl.when((z == 1) | (z == 2))
        def _():
            for h in (0, 1):
                for rg in range(4):
                    ph(s, rg, h, up).start()

        gram(s, (0, 1))

    def third(s, up):
        for h in (0, 1):
            for rg in range(4):
                ph(s, rg, h, up).wait_recv()
            gram(s, (h,))

    def each(d, fn):
        @pl.when(z - d >= 0)
        def _():
            fn(z - d, True)

        @pl.when(z + d <= 3)
        def _():
            fn(z + d, False)

    for i in range(4):
        near(i)
        r = order(z, i)
        px(0, c, r).wait_recv()
        px(2, xn, r).start()
    for i in range(4):
        px(1, c, i).wait_recv()
        px(2, c, i).wait_recv()
    gram(z, (0, 1))
    each(1, lambda s, up: gram(s, (0, 1)))
    each(2, second)
    finish(z)
    each(1, lambda s, up: finish(s))
    each(3, third)
    each(2, lambda s, up: finish(s))
    each(3, lambda s, up: finish(s))

    for r in range(4):
        for kc in range(r + 1):
            @pl.when((r <= z) & (z < 3))
            def _():
                t_up(r, kc).wait_send()

            @pl.when((r >= z) & (z > 0))
            def _():
                t_dn(r, kc).wait_send()

            t_xn(r, kc).wait_send()
            t_sib(r, kc).wait_send()
            t_fwd(r, kc).wait_send()
        for s in range(4):
            @pl.when((s <= z) & (z < 3) & (z - s < 2))
            def _():
                pz(s, r, True).wait_send()

            @pl.when((s >= z) & (z > 0) & (s - z < 2))
            def _():
                pz(s, r, False).wait_send()

        px(0, c, r).wait_send()
        px(1, c, r).wait_send()
        px(2, xn, r).wait_send()
        for h in (0, 1):
            @pl.when((z == 1) | (z == 2))
            def _():
                ph(3, r, h, False).wait_send()

            emit(r, h).wait()


LIMIT = 204


def body(groups, factor, pivots, constraints):
    nb, piece, order_m = factor.shape
    strip = constraints.shape[2]
    assert strip == W and order_m == 4 * W and piece * 4 == W
    dma = pltpu.SemaphoreType.DMA
    wide = [
        pltpu.VMEM((4, nb, 4 * W, W), f32),
        pltpu.VMEM((nb, 4 * W, W), f32),
        pltpu.VMEM((nb, 4 * W, W), bf16),
        pltpu.VMEM((nb, 4 * W, W), bf16),
        pltpu.VMEM((W, W), f32),
    ]
    vmem, anywhere = pl.BlockSpec(memory_space=pltpu.VMEM), pl.BlockSpec(memory_space=pl.ANY)
    if groups == 2:
        kernel, rows_out, limit = paired, 2 * W, LIMIT
        in_specs, out_specs = [vmem, vmem, anywhere], vmem
        scratch = wide + [
            pltpu.VMEM((2, W, W), f32),
            pltpu.VMEM((4, 4, nb * W, W), bf16),
            pltpu.VMEM((4, 4, W, nb * W), bf16),
            pltpu.VMEM((4, 4, W, nb * W), bf16),
            pltpu.VMEM((4, 2, 2, W + 16, H), bf16),
            pltpu.VMEM((4, 2, 2, W + 16, H), bf16),
            pltpu.VMEM((2, 2, 2, 2, W + 16, H), bf16),
            pltpu.VMEM((2, 2, 2, 2, W + 16, H), bf16),
            pltpu.VMEM((2, 2, 2, W + 16, H), bf16),
            dma,
            dma((5, 4, 4, nb)),
            dma((4, 4, 4, nb)),
            dma((4, nb)),
            dma((4, 4, nb)),
            dma((4, nb)),
            dma((4, nb)),
            dma((4, nb, 2)),
            dma((4, nb, 2)),
            dma((3, 4, nb, 2)),
            dma((3, 4, nb, 2)),
            dma((4, nb, 2)),
            dma((4, nb, 2)),
            dma((2, 4, nb, 2)),
            dma((2, 4, nb, 2)),
            dma((4, 2, 2)),
            dma((4, 2, 2)),
            dma((2, 2, 2, 2)),
            dma((2, 2, 2, 2)),
            dma((2, 2, 2)),
            dma((2, 2, 2)),
        ]
    else:
        kernel, rows_out, limit = single, 4 * W, 208
        pivots = jnp.tile(pivots, (1, 4))
        in_specs, out_specs = [vmem, vmem, anywhere], anywhere
        scratch = wide + [
            pltpu.VMEM((4, 4, nb * W, W), bf16),
            pltpu.VMEM((4, 4, W, nb * W), bf16),
            pltpu.VMEM((rows_out, 4 * W), f32),
            dma,
            dma((5, 4, 4)),
            dma((4, 4, 4)),
            dma((2, 4, 4)),
            dma((4, 4)),
            dma((4, 2)),
            dma((4, 2)),
            dma((3, 4)),
            dma((3, 4)),
            dma((4, 2)),
        ]
    result = pl.pallas_call(
        functools.partial(kernel, nb),
        out_shape=jax.ShapeDtypeStruct((rows_out, 4 * W), f32),
        in_specs=in_specs,
        out_specs=out_specs,
        scratch_shapes=scratch,
        compiler_params=pltpu.CompilerParams(
            collective_id=0, has_side_effects=True, vmem_limit_bytes=limit << 18),
    )(factor, pivots, constraints)
    if groups != 2:
        result = lax.psum_scatter(result, "grp", scatter_dimension=0, tiled=True)
    return result[None]


def solution(mesh):
    in_specs = (
        P("grp", ("row", "col"), None),
        P("grp", ("row", "col")),
        P("grp", None, ("col", "row")),
    )
    return jax.shard_map(
        functools.partial(body, mesh.shape["grp"]), mesh=mesh, in_specs=in_specs,
        out_specs=P("row", "grp", "col"), check_vma=False)
```
